512 devices in a mesh: seg: 32 (over z, core), fsdp: 16 (over y, x).
Axes of the slice: x: 4, y: 4, z: 16, core: 2. Of those that a mesh axis runs over, the one named last changes fastest.
Arguments:
- frames: bfloat16 [16, 256, 16, 1024], P('fsdp', 'seg'), may hold values from -6 to 6
- memory_in: bfloat16 [16, 256, 1024], P('fsdp', 'seg'), may hold values from -6 to 6
- lengths: int32 [16], P('fsdp'), may hold values from 1 to 256, as said below
- ln_gain: float32 [1024], replicated, may hold values from 0.25 to 1.75
- w_query: bfloat16 [1024, 1024], P('fsdp'), may hold values from -1 to 1
- w_key: bfloat16 [1024, 1024], P('fsdp'), may hold values from -12 to 12
- w_value: bfloat16 [1024, 1024], P('fsdp'), may hold values from -0.1875 to 0.1875
- w_out: bfloat16 [1024, 1024], P('fsdp'), may hold values from -0.1875 to 0.1875
- grad_frames: bfloat16 [16, 256, 16, 1024], P('fsdp', 'seg'), may hold values from -6 to 6
- grad_memory: bfloat16 [16, 256, 1024], P('fsdp', 'seg'), may hold values from -6 to 6
Outputs:
- frames_out: bfloat16 [16, 256, 16, 1024], P('fsdp', 'seg')
- memory_out: bfloat16 [16, 256, 1024], P('fsdp', 'seg')
- value_grad: float32 [1024, 1024], P('fsdp')
The draws below stay inside these ranges and needn't reach their ends.
Inputs may be any that keep to these rules, and one draw needn't show every extreme that they name: `lengths`: in every aligned block of 1 utterances (those of one fsdp index) at least one has length 256.
All inputs are finite; a program needn't handle non-finite values.
Results may differ from the reference program's by a relative error of at most 0.04.
Values may be sent and summed in bfloat16 or wider, within the bound.
A program may use at most 64 MiB of HBM per device.

```python
import math
import jax
import jax.numpy as jnp
from jax import lax

D = 1024
HEADS = 16
FRAMES = 16
LEFT = 16
MEMORY = 8
UTT_DEV = 1
UTT = 16
SEGS = 256
KEYS = 40


def projection_pair(key):
    base_matrix = jax.random.normal(jax.random.fold_in(key, 101), (D, D), jnp.float32) / math.sqrt(D)
    other_matrix = jax.random.normal(jax.random.fold_in(key, 202), (D, D), jnp.float32) / math.sqrt(D)
    keyed = other_matrix
    return (jnp.clip(base_matrix, -1.0, 1.0), jnp.clip(keyed, -12.0, 12.0))


def draw_w_query(key, part):
    return projection_pair(key)[0].astype(jnp.bfloat16)


def draw_w_key(key, part):
    return projection_pair(key)[1].astype(jnp.bfloat16)


def draw_lengths(key, part):
    picked = jax.random.randint(jax.random.fold_in(key, 7), (UTT,), 1, SEGS + 1)
    full_slot = jax.random.randint(jax.random.fold_in(key, 8), (UTT // UTT_DEV, 1), 0, UTT_DEV)
    is_full = (jnp.arange(UTT_DEV)[None, :] == full_slot).reshape(UTT)
    return jnp.where(is_full, SEGS, picked).astype(jnp.int32)


def levels(key, extent, shards, least, largest):
    loudness = 1.0
    for axis_at, parts in shards:
        draws = jax.random.uniform(jax.random.fold_in(jax.random.fold_in(key, 6), axis_at), (parts,), jnp.float32, least / len(shards), largest / len(shards))
        loudness = loudness * jnp.repeat(jnp.exp(draws), extent[axis_at] // parts).reshape((-1,) + (1,) * (len(extent) - 1 - axis_at))
    return loudness


def gaussian(rng, extent, width, reach, split=(), held_as=jnp.bfloat16):
    entries = jax.random.normal(rng, extent, jnp.float32) * width
    if len(split) > 0:
        entries = levels(rng, extent, split, -0.22, 0.18) * entries
    return jnp.clip(entries, min=-reach, max=reach).astype(held_as)


def setup_inputs(seed: int = 0) -> dict:
    keys = jax.random.split(jax.random.key(seed), 11)
    frames = gaussian(keys[0], (UTT, SEGS, FRAMES, D), 1.0, 6.0, ((0, 16), (1, 32)))
    memory_in = gaussian(keys[1], (UTT, SEGS, D), 1.0, 6.0, ((0, 16), (1, 32)))
    lengths = draw_lengths(jax.random.fold_in(keys[10], 71), 0)
    ln_gain = jnp.clip(1.0 + 0.15 * jax.random.normal(keys[3], (D,), jnp.float32), 0.25, 1.75)
    w_query = draw_w_query(jax.random.fold_in(keys[10], 71), 0)
    w_key = draw_w_key(jax.random.fold_in(keys[10], 71), 0)
    w_value = gaussian(keys[6], (D, D), D ** -0.5, 0.1875, ((0, 16),))
    w_out = gaussian(keys[7], (D, D), D ** -0.5, 0.1875, ((0, 16),))
    grad_frames = gaussian(keys[8], (UTT, SEGS, FRAMES, D), 1.0, 6.0, ((0, 16), (1, 32)))
    grad_memory = gaussian(keys[9], (UTT, SEGS, D), 1.0, 6.0, ((0, 16), (1, 32)))
    return dict(frames=frames, memory_in=memory_in, lengths=lengths, ln_gain=ln_gain, w_query=w_query, w_key=w_key, w_value=w_value, w_out=w_out, grad_frames=grad_frames, grad_memory=grad_memory)


epsilon = 1e-05
masked_score = -1e+30

def reference(frames, memory_in, lengths, ln_gain, w_query, w_key, w_value, w_out, grad_frames, grad_memory):
    head_dim = D // HEADS
    query_count = FRAMES + 1

    def per_utterance(running, sliced):
        utter_frames, utter_memory, utter_length, utter_grad, memory_grad = sliced
        seg_count = utter_frames.shape[0]
        wide_frames = utter_frames.astype(jnp.float32)
        row_mean = lax.optimization_barrier(jnp.mean(wide_frames, axis=-1, keepdims=True))
        centred = wide_frames - row_mean
        row_var = lax.optimization_barrier(jnp.mean(centred * centred, axis=-1, keepdims=True))
        normed = (centred * lax.rsqrt(row_var + epsilon) * ln_gain).astype(jnp.bfloat16)
        summary = lax.optimization_barrier(jnp.mean(normed.astype(jnp.float32), axis=1)).astype(jnp.bfloat16)
        query_rows = jnp.concatenate([normed, summary[:, None, :]], axis=1)
        queries = jnp.dot(query_rows.reshape(-1, D), w_query, preferred_element_type=jnp.float32).astype(jnp.bfloat16)
        queries = queries.reshape(seg_count, query_count, HEADS, head_dim).astype(jnp.float32)
        flat_normed = normed.reshape(-1, D)
        own_key = jnp.dot(flat_normed, w_key, preferred_element_type=jnp.float32).astype(jnp.bfloat16).reshape(seg_count, FRAMES, D)
        own_value = jnp.dot(flat_normed, w_value, preferred_element_type=jnp.float32).astype(jnp.bfloat16).reshape(seg_count, FRAMES, D)
        memory_key = jnp.dot(utter_memory, w_key, preferred_element_type=jnp.float32).astype(jnp.bfloat16)
        memory_value = jnp.dot(utter_memory, w_value, preferred_element_type=jnp.float32).astype(jnp.bfloat16)
        position = jnp.arange(seg_count).astype(jnp.int32)
        source = position[:, None] - 1 - jnp.arange(MEMORY).astype(jnp.int32)[None, :]
        memory_valid = source >= 0
        clipped = jnp.clip(source, 0, seg_count - 1).astype(jnp.int32)

        def window(table):
            return jnp.where(memory_valid[:, :, None], table[clipped], jnp.zeros((), table.dtype))

        def previous(block):
            return jnp.concatenate([jnp.zeros((1, LEFT, D), block.dtype), block[:-1, FRAMES - LEFT:]], axis=0)
        key_proj = jnp.concatenate([window(memory_key), previous(own_key), own_key], axis=1)
        value_proj = jnp.concatenate([window(memory_value), previous(own_value), own_value], axis=1)
        key_proj = key_proj.reshape(seg_count, KEYS, HEADS, head_dim).astype(jnp.float32)
        value_proj = value_proj.reshape(seg_count, KEYS, HEADS, head_dim).astype(jnp.float32)
        scores = jnp.einsum('sqhd,skhd->shqk', queries, key_proj) / math.sqrt(head_dim)
        left_valid = jnp.broadcast_to((position >= 1)[:, None], (seg_count, LEFT))
        own_valid = jnp.ones((seg_count, FRAMES), dtype=bool)
        valid_key = jnp.concatenate([memory_valid, left_valid, own_valid], axis=1)
        scores = jnp.where(valid_key[:, None, None, :], scores, masked_score)
        highest = lax.optimization_barrier(jnp.max(scores, axis=-1, keepdims=True))
        exponent = jnp.exp(scores - highest)
        soft_weights = (exponent / lax.optimization_barrier(jnp.sum(exponent, axis=-1, keepdims=True))).astype(jnp.bfloat16).astype(jnp.float32)
        attended = jnp.einsum('shqk,skhd->sqhd', soft_weights, value_proj).astype(jnp.bfloat16).reshape(-1, D)
        projected = jnp.dot(attended, w_out, preferred_element_type=jnp.float32).reshape(seg_count, query_count, D)
        live_mask = (position < utter_length).astype(jnp.float32)
        out_frames = (wide_frames + live_mask[:, None, None] * projected[:, :FRAMES]).astype(jnp.bfloat16)
        out_memory = (live_mask[:, None] * projected[:, FRAMES]).astype(jnp.bfloat16)
        upstream = jnp.concatenate([utter_grad, memory_grad[:, None, :]], axis=1).reshape(-1, D)
        back_proj = jnp.dot(upstream, w_out.T, preferred_element_type=jnp.float32).reshape(seg_count, query_count, D)
        grad_attended = (live_mask[:, None, None] * back_proj).astype(jnp.bfloat16)
        grad_attended = grad_attended.reshape(seg_count, query_count, HEADS, head_dim).astype(jnp.float32)
        grad_values = jnp.einsum('shqk,sqhd->skhd', soft_weights, grad_attended).astype(jnp.bfloat16)
        grad_values = grad_values.astype(jnp.float32).reshape(seg_count, KEYS, D)
        own_total = grad_values[:, MEMORY + LEFT:]
        own_total = own_total.at[:-1, FRAMES - LEFT:].add(grad_values[1:, MEMORY:MEMORY + LEFT])
        memory_total = jnp.zeros((seg_count, D), jnp.float32)
        for memory_slot in range(MEMORY):
            padded = jnp.concatenate([grad_values[:, memory_slot], jnp.zeros((1 + memory_slot, D), jnp.float32)], axis=0)
            memory_total = memory_total + padded[1 + memory_slot:1 + memory_slot + seg_count]
        grad_term = jnp.dot(flat_normed.astype(jnp.float32).T, own_total.reshape(-1, D), precision=lax.Precision.HIGHEST)
        grad_term = grad_term + jnp.dot(utter_memory.astype(jnp.float32).T, memory_total, precision=lax.Precision.HIGHEST)
        return (running + grad_term, (out_frames, out_memory))
    zero_grad = jnp.zeros((D, D), jnp.float32)
    value_grad, outputs = lax.scan(per_utterance, zero_grad, (frames, memory_in, lengths, grad_frames, grad_memory))
    return (outputs[0], outputs[1], value_grad)
```

```python
import functools

import jax
import jax.numpy as jnp
from jax import lax
from jax.experimental import pallas as pl
from jax.experimental.pallas import tpu as pltpu
from jax.sharding import PartitionSpec as P

F32 = jnp.float32
BF16 = jnp.bfloat16
MESH = pl.DeviceIdType.MESH
EPSILON = 1e-05
MASKED = -1e30
KEY, QUERY, OUT, VALUE = 0, 1, 2, 3
N_REMOTE = 120
N_LOCAL = 16


def mm(a, b):
    return jnp.dot(a, b, preferred_element_type=F32)


def kernel(
    frames, memory, lengths, gain, w_query, w_key, w_value, w_out, grad_frames, grad_memory,
    frames_out, memory_out, value_grad,
    W, WO2, fin, gin, mem, gmem, E, U, L, X, XT, bias, K, Q, V, PT, GA, GV, ATT, PP, PPR,
    G, RA1, RA2A, RA2B, SA, RS, RF, RB1, RB2A, RB2B, SB, T, ZS, ZR, ZQ, OB,
    fo_v, mo_v, gain_v,
    send_sem, recv_sem, local_sem,
):
    seg = lax.axis_index("seg")
    fsdp = lax.axis_index("fsdp")
    core = lax.rem(seg, 2)
    z = lax.div(seg, 2)
    x = lax.rem(fsdp, 4)
    y = lax.div(fsdp, 4)
    other = 1 - core
    quad = lax.div(z, 4)
    place = lax.rem(z, 4)

    def wrap(a, by, n=4):
        return lax.rem(a + by + n, n)

    def device(dx=0, dy=0, dz=0, flip=False, quad_by=None):
        c = other if flip else core
        if quad_by is None:
            zz = wrap(z, dz, 16)
        else:
            zz = quad * 4 + wrap(place, quad_by)
        return (zz * 2 + c, wrap(y, dy) * 4 + wrap(x, dx))

    counter = [0]

    def remote(src, dst, to):
        i = counter[0]
        counter[0] += 1
        copy = pltpu.make_async_remote_copy(
            src_ref=src, dst_ref=dst, send_sem=send_sem.at[i], recv_sem=recv_sem.at[i],
            device_id=to, device_id_type=MESH,
        )
        copy.start()
        sent.append(copy)
        return copy

    sent = []
    lcounter = [0]

    def local(src, dst):
        i = lcounter[0]
        lcounter[0] += 1
        copy = pltpu.make_async_copy(src, dst, local_sem.at[i])
        copy.start()
        return copy

    weights = (w_key, w_query, w_out, w_value)
    own_columns = pl.ds(pl.multiple_of(core * 512, 512), 512)
    own = []
    for m in range(4):
        own.append([
            local(weights[m].at[pl.ds(32 * d, 32), own_columns], W.at[m, y, x, d])
            for d in range(2)
        ])
    in_frames = local(frames, fin)
    in_gain = local(gain, gain_v)
    in_mem = local(memory, mem)
    in_grad = local(grad_frames, gin)
    in_gmem = local(grad_memory, gmem)

    partners = [device(dx=1), device(dx=-1), device(dy=1), device(dy=-1), device(flip=True)]
    partners += [device(dz=1), device(dz=-1), device(dz=4), device(dz=-4)]
    for k in (1, 2, 3):
        partners += [device(quad_by=k), device(quad_by=k, flip=True)]
    barrier = pltpu.get_barrier_semaphore()
    for partner in partners:
        pl.semaphore_signal(barrier, inc=1, device_id=partner, device_id_type=MESH)
    pl.semaphore_wait(barrier, len(partners))

    def first_to(d, s):
        return device(dx=s) if d == 0 else device(dy=s)

    def second_to(d, s):
        return device(dy=s) if d == 0 else device(dx=s)

    def ring_one(m):
        return {(d, s): remote(W.at[m, y, x, d], W.at[m, y, x, d], first_to(d, s))
                for s in (1, -1) for d in (0, 1)}

    def relay_one(m, came):
        out = {}
        for s in (1, -1):
            for d in (0, 1):
                came[d, s].wait_recv()
                rows = pl.ds(0 if s == 1 else 16, 16)
                ref = (W.at[m, y, wrap(x, -s), 0, rows] if d == 0
                       else W.at[m, wrap(y, -s), x, 1, rows])
                out[d, s] = remote(ref, ref, first_to(d, s))
        return out

    def ring_two(m, came):
        out = {}
        for d in (0, 1):
            for s in (1, -1):
                came[d, s].wait_recv()
        for s in (1, -1):
            for d in (0, 1):
                ref = W.at[m, y, :, 0] if d == 0 else W.at[m, :, x, 1]
                out[d, s] = remote(ref, ref, second_to(d, s))
        return out

    def relay_two(m, came):
        out = {}
        for s in (1, -1):
            for d in (0, 1):
                came[d, s].wait_recv()
                half = pl.ds(0 if s == 1 else 2, 2)
                ref = (W.at[m, wrap(y, -s), half, 0] if d == 0
                       else W.at[m, half, wrap(x, -s), 1])
                out[d, s] = remote(ref, ref, second_to(d, s))
        return out

    def finish(came):
        for s in (1, -1):
            for d in (0, 1):
                came[d, s].wait_recv()

    def weight(m):
        return W[m].reshape(1024, 512)

    one, one_relayed, two, two_relayed = {}, {}, {}, {}
    for m in range(4):
        for copy in own[m]:
            copy.wait()
        one[m] = ring_one(m)

    in_frames.wait()
    in_gain.wait()
    in_mem.wait()
    sums = []
    for t in range(8):
        rows = fin[16 * t:16 * t + 16, :].astype(F32)
        centred = rows - jnp.mean(rows, axis=-1, keepdims=True)
        var = jnp.mean(centred * centred, axis=-1, keepdims=True)
        normed = (centred * lax.rsqrt(var + EPSILON) * gain_v[...]).astype(BF16)
        E[core, 16 * t:16 * t + 16, :] = normed
        sums.append(jnp.mean(normed.astype(F32), axis=0, keepdims=True))
    zeros8 = jnp.zeros((8, 1024), F32)
    E[core, 128:144, :] = jnp.concatenate(sums + [zeros8], axis=0).astype(BF16)
    E[core, 144:160, :] = jnp.concatenate([mem[...].astype(F32), zeros8], axis=0).astype(BF16)
    rows_over = remote(E.at[core], E.at[core], device(flip=True))

    for m in range(4):
        one_relayed[m] = relay_one(m, one[m])

    in_grad.wait()
    in_gmem.wait()
    for h in range(2):
        cols = slice(512 * h, 512 * h + 512)
        U[core, h, 0:128, :] = gin[:, cols]
        U[core, h, 128:144, :] = jnp.concatenate(
            [gmem[:, cols].astype(F32), zeros8[:, :512]], axis=0).astype(BF16)
    grads_over = remote(U.at[core], U.at[core], device(flip=True))

    two[0] = ring_two(0, one_relayed[0])
    two[1] = ring_two(1, one_relayed[1])
    rows_over.wait_recv()
    tail_over = remote(E.at[1, 112:128], L.at[0], device(dz=1))
    bank_over = remote(E.at[1, 144:160], L.at[1], device(dz=1))

    slot = lax.broadcasted_iota(jnp.int32, (160, 144), 0)
    column = lax.broadcasted_iota(jnp.int32, (160, 144), 1)
    query_at = jnp.where(column < 128, column // 16, column - 128)
    key_at = jnp.where(slot < 144, slot // 16 - 1, slot - 152)
    reach = jnp.where(slot < 144, 1, 8)
    newest = jnp.where(slot < 144, 0, 1)
    back = query_at - key_at
    for g in range(2):
        base = (2 * z + g) * 8
        valid = (back >= newest) & (back <= reach) & (key_at + base >= 0)
        bias[g] = jnp.where(valid, 0.0, MASKED).astype(F32)

    X[0, 16:144, :] = E[0, 0:128, :]
    X[1, 16:144, :] = E[1, 0:128, :]
    X[1, 0:16, :] = E[0, 112:128, :]
    bank0 = E[0, 144:160, :].astype(F32)[:8]
    bank1 = E[1, 144:160, :].astype(F32)[:8]
    X[1, 144:160, :] = jnp.concatenate([bank0, bank1], axis=0).astype(BF16)
    tail_over.wait_recv()
    bank_over.wait_recv()
    X[0, 0:16, :] = L[0]
    X[0, 144:160, :] = jnp.concatenate([L[1].astype(F32)[:8], bank0], axis=0).astype(BF16)
    for k in range(4):
        cols = slice(256 * k, 256 * k + 256)
        block = X[:, :, cols].reshape(320, 256).astype(F32)
        block = jnp.concatenate([block, jnp.zeros((64, 256), F32)], axis=0)
        XT[cols, :] = block.T.astype(BF16)

    two_relayed[0] = relay_two(0, two[0])
    two[2] = ring_two(2, one_relayed[2])

    low = lax.broadcasted_iota(jnp.int32, (1, 128), 1) < 64

    def split_heads(dst, value, g, p):
        dst[g, p, 0:160, :] = jnp.where(low, value, 0.0).astype(BF16)
        dst[g, p, 160:320, :] = jnp.where(low, 0.0, value).astype(BF16)

    def project_keys(m, dst):
        rows = X[...].reshape(320, 1024)
        for n in range(2):
            w = W[m, :, :, :, :, 256 * n:256 * n + 256].reshape(1024, 256)
            out = mm(rows, w)
            for g in range(2):
                for p in range(2):
                    split_heads(dst, out[160 * g:160 * g + 160, 128 * p:128 * p + 128], g, 2 * n + p)

    finish(two_relayed[0])
    project_keys(KEY, K)

    two_relayed[1] = relay_two(1, two[1])
    two_relayed[2] = relay_two(2, two[2])
    two[3] = ring_two(3, one_relayed[3])
    finish(two_relayed[1])
    query_rows = E[:, 0:144, :].reshape(288, 1024)
    for n in range(2):
        w = W[QUERY, :, :, :, :, 256 * n:256 * n + 256].reshape(1024, 256)
        out = mm(query_rows, w).astype(BF16)
        for g in range(2):
            for p in range(2):
                Q[g, 2 * n + p] = out[144 * g:144 * g + 144, 128 * p:128 * p + 128]

    def attend(i, carry):
        g = lax.div(i, 4)
        p = lax.rem(i, 4)
        scores = lax.dot_general(
            K[g, p], Q[g, p], (((1,), (1,)), ((), ())), preferred_element_type=F32)
        for h in range(2):
            s = scores[160 * h:160 * h + 160] * 0.125 + bias[g]
            e = jnp.exp(s - jnp.max(s, axis=0, keepdims=True))
            total = jnp.sum(e, axis=0, keepdims=True)
            PT[g, p, 160 * h:160 * h + 160, :] = (e / total).astype(BF16)
        return carry

    lax.fori_loop(0, 8, attend, 0)

    finish(two_relayed[2])
    out_over = remote(W.at[OUT, pl.ds(2 * other, 2)], WO2.at[core], device(flip=True))
    out_here = local(W.at[OUT, pl.ds(2 * core, 2)], WO2.at[core])
    grads_over.wait_recv()
    out_here.wait()
    out_over.wait_recv()

    def live_of(g, shape):
        r = lax.broadcasted_iota(jnp.int32, shape, 0)
        at = jnp.where(r < 128, r // 16, r - 128)
        return jnp.where((2 * z + g) * 8 + at < lengths[0], 1.0, 0.0).astype(F32)

    for g in range(2):
        ga = jnp.zeros((144, 512), F32)
        for h in range(2):
            w = WO2[h].reshape(512, 512)
            ga = ga + lax.dot_general(
                U[g, h], w, (((1,), (1,)), ((), ())), preferred_element_type=F32)
        ga = (ga * live_of(g, (144, 1))).astype(BF16)
        for p in range(4):
            GA[g, p] = ga[:, 128 * p:128 * p + 128]

    for g in range(2):
        for p in range(4):
            both = mm(PT[g, p], GA[g, p])
            GV[160 * g:160 * g + 160, 128 * p:128 * p + 128] = jnp.where(
                low, both[0:160], both[160:320]).astype(BF16)
    GV[320:384, :] = jnp.zeros((64, 512), BF16)

    def grad_rows(i, carry):
        block = mm(XT[pl.ds(pl.multiple_of(i * 256, 256), 256), :], GV[...])
        G[i] = block.astype(BF16).reshape(4, 2, 32, 512)
        return carry

    lax.fori_loop(0, 4, grad_rows, 0)

    def a_to(d, s):
        return device(dy=s) if d == 0 else device(dx=s)

    def b_to(d, s):
        return device(dx=s) if d == 0 else device(dy=s)

    a_at = (y, x)
    b_at = (x, y)

    def g_part(d, a, h):
        return (a, pl.ds(2 * h, 2), 0) if d == 0 else (pl.ds(2 * h, 2), a, 1)

    ways = [(d, s) for s in (1, -1) for d in (0, 1)]
    half_of = {1: 0, -1: 1}
    a1, a2a, a2b = {}, {}, {}
    for d, s in ways:
        h = half_of[s]
        a1[d, s] = remote(G.at[g_part(d, wrap(a_at[d], 2), h)], RA1.at[d, h], a_to(d, s))
    for d, s in ways:
        h = half_of[s]
        a2b[d, s] = remote(G.at[g_part(d, wrap(a_at[d], s), 1 - h)], RA2B.at[d, h], a_to(d, s))
    for d, s in ways:
        h = half_of[s]
        a1[d, s].wait_recv()
        SA[d, h] = (G[g_part(d, wrap(a_at[d], s), h)].astype(F32) + RA1[d, h].astype(F32)).astype(BF16)
        a2a[d, s] = remote(SA.at[d, h], RA2A.at[d, h], a_to(d, s))

    two_relayed[3] = relay_two(3, two[3])

    b1, b2a, b2b = {}, {}, {}
    for d in range(2):
        for s in (1, -1):
            a2a[d, s].wait_recv()
            a2b[d, s].wait_recv()
        for h in range(2):
            total = (G[g_part(d, a_at[d], h)].astype(F32) + RA2A[d, h].astype(F32)
                     + RA2B[d, 1 - h].astype(F32))
            RF[d, 2 * h:2 * h + 2] = total.reshape(2, 2, 16, 512)
            RS[d, 2 * h:2 * h + 2] = total.astype(BF16).reshape(2, 2, 16, 512)
        for s in (1, -1):
            h = half_of[s]
            b1[d, s] = remote(RS.at[d, wrap(b_at[d], 2), h], RB1.at[d, h], b_to(d, s))
            b2b[d, s] = remote(RS.at[d, wrap(b_at[d], s), 1 - h], RB2B.at[d, h], b_to(d, s))
    for d, s in ways:
        h = half_of[s]
        b1[d, s].wait_recv()
        SB[d, h] = (RF[d, wrap(b_at[d], s), h] + RB1[d, h].astype(F32)).astype(BF16)
        b2a[d, s] = remote(SB.at[d, h], RB2A.at[d, h], b_to(d, s))
    for d in range(2):
        for s in (1, -1):
            b2a[d, s].wait_recv()
            b2b[d, s].wait_recv()
        for h in range(2):
            total = RF[d, b_at[d], h] + RB2A[d, h].astype(F32) + RB2B[d, 1 - h].astype(F32)
            T[2 * d + h] = total
            ZS[2 * d + h] = total.astype(BF16)

    z1 = [remote(ZS.at[wrap(place, k)], ZR.at[k - 1], device(quad_by=k)) for k in (1, 2, 3)]

    finish(two_relayed[3])
    project_keys(VALUE, V)

    for copy in z1:
        copy.wait_recv()
    part = T[place]
    for k in range(3):
        part = part + ZR[k].astype(F32)
    ZQ[quad] = part.astype(BF16)
    z2 = {s: remote(ZQ.at[quad], ZQ.at[quad], device(dz=4 * s)) for s in (1, -1)}

    def attended(i, carry):
        g = lax.div(i, 4)
        p = lax.rem(i, 4)
        ATT[g, p] = lax.dot_general(
            PT[g, p], V[g, p], (((0,), (0,)), ((), ())), preferred_element_type=F32).astype(BF16)
        return carry

    lax.fori_loop(0, 8, attended, 0)

    z3 = {}
    for s in (1, -1):
        z2[s].wait_recv()
        cols = pl.ds(256 * half_of[s], 256)
        ref = ZQ.at[wrap(quad, -s), :, cols]
        z3[s] = remote(ref, ref, device(dz=4 * s))

    def project(g, h):
        rows = jnp.concatenate([ATT[g, p] for p in range(4)], axis=1)
        return mm(rows, WO2[h].reshape(512, 512))

    for h in range(2):
        PP[h] = project(other, h).astype(BF16)
    projected_over = remote(PP, PPR, device(flip=True))

    for s in (1, -1):
        z3[s].wait_recv()
    done = ((ZQ[0].astype(F32) + ZQ[1].astype(F32)) + ZQ[2].astype(F32)) + ZQ[3].astype(F32)
    OB[core, place] = done.astype(BF16)
    mine = OB.at[core, place]
    z4 = [remote(mine, mine, device(quad_by=k)) for k in (1, 2, 3)]
    z4 += [remote(mine, mine, device(quad_by=k, flip=True)) for k in (0, 1, 2, 3)]

    projected_over.wait_recv()
    live = live_of(core, (144, 1))
    for h in range(2):
        cols = slice(512 * h, 512 * h + 512)
        out = (project(core, h) + PPR[h].astype(F32)) * live
        fo_v[:, cols] = (fin[:, cols].astype(F32) + out[0:128]).astype(BF16)
        mo_v[:, cols] = out[128:136].astype(BF16)
    put_frames = local(fo_v, frames_out)
    put_memory = local(mo_v, memory_out)

    for copy in z4:
        copy.wait_recv()
    for h in range(2):
        value_grad[:, 512 * h:512 * h + 512] = OB[h].astype(F32).reshape(64, 512)
    put_frames.wait()
    put_memory.wait()
    for copy in sent:
        copy.wait_send()


def on_device(
    frames, memory_in, lengths, ln_gain, w_query, w_key, w_value, w_out, grad_frames, grad_memory
):
    any_spec = pl.BlockSpec(memory_space=pl.ANY)
    vmem = pltpu.VMEM
    scratch = [
        vmem((4, 4, 4, 2, 32, 512), BF16),
        vmem((2, 2, 4, 2, 32, 512), BF16),
        vmem((128, 1024), BF16),
        vmem((128, 1024), BF16),
        vmem((8, 1024), BF16),
        vmem((8, 1024), BF16),
        vmem((2, 160, 1024), BF16),
        vmem((2, 2, 144, 512), BF16),
        vmem((2, 16, 1024), BF16),
        vmem((2, 160, 1024), BF16),
        vmem((1024, 384), BF16),
        vmem((2, 160, 144), F32),
        vmem((2, 4, 320, 128), BF16),
        vmem((2, 4, 144, 128), BF16),
        vmem((2, 4, 320, 128), BF16),
        vmem((2, 4, 320, 144), BF16),
        vmem((2, 4, 144, 128), BF16),
        vmem((384, 512), BF16),
        vmem((2, 4, 144, 128), BF16),
        vmem((2, 144, 512), BF16),
        vmem((2, 144, 512), BF16),
        vmem((4, 4, 2, 32, 512), BF16),
        vmem((2, 2, 2, 32, 512), BF16),
        vmem((2, 2, 2, 32, 512), BF16),
        vmem((2, 2, 2, 32, 512), BF16),
        vmem((2, 2, 2, 32, 512), BF16),
        vmem((2, 4, 2, 16, 512), BF16),
        vmem((2, 4, 2, 16, 512), F32),
        vmem((2, 2, 16, 512), BF16),
        vmem((2, 2, 16, 512), BF16),
        vmem((2, 2, 16, 512), BF16),
        vmem((2, 2, 16, 512), BF16),
        vmem((4, 16, 512), F32),
        vmem((4, 16, 512), BF16),
        vmem((3, 16, 512), BF16),
        vmem((4, 16, 512), BF16),
        vmem((2, 4, 16, 512), BF16),
        vmem((128, 1024), BF16),
        vmem((8, 1024), BF16),
        vmem((1, 1024), F32),
        pltpu.SemaphoreType.DMA((N_REMOTE,)),
        pltpu.SemaphoreType.DMA((N_REMOTE,)),
        pltpu.SemaphoreType.DMA((N_LOCAL,)),
    ]
    frames_out, memory_out, value_grad = pl.pallas_call(
        kernel,
        out_shape=(
            jax.ShapeDtypeStruct((128, 1024), BF16),
            jax.ShapeDtypeStruct((8, 1024), BF16),
            jax.ShapeDtypeStruct((64, 1024), F32),
        ),
        in_specs=[any_spec, any_spec, pl.BlockSpec(memory_space=pltpu.SMEM)] + [any_spec] * 7,
        out_specs=(any_spec, any_spec, pl.BlockSpec(memory_space=vmem)),
        scratch_shapes=scratch,
        compiler_params=pltpu.CompilerParams(
            collective_id=0, has_side_effects=True, vmem_limit_bytes=48 * 1024 * 1024
        ),
    )(
        frames.reshape(128, 1024), memory_in.reshape(8, 1024), lengths, ln_gain.reshape(1, 1024),
        w_query, w_key, w_value, w_out,
        grad_frames.reshape(128, 1024), grad_memory.reshape(8, 1024),
    )
    return (frames_out.reshape(frames.shape), memory_out.reshape(memory_in.shape), value_grad)


def solution(mesh):
    return jax.shard_map(
        on_device,
        mesh=mesh,
        in_specs=(
            P("fsdp", "seg", None, None),
            P("fsdp", "seg", None),
            P("fsdp"),
            P(),
            P("fsdp", None),
            P("fsdp", None),
            P("fsdp", None),
            P("fsdp", None),
            P("fsdp", "seg", None, None),
            P("fsdp", "seg", None),
        ),
        out_specs=(P("fsdp", "seg", None, None), P("fsdp", "seg", None), P("fsdp", None)),
        check_vma=False,
    )
```

```python
import functools

import jax
import jax.numpy as jnp
from jax import lax
from jax.experimental import pallas as pl
from jax.experimental.pallas import tpu as pltpu
from jax.sharding import PartitionSpec as P

F32 = jnp.float32
BF16 = jnp.bfloat16
MESH = pl.DeviceIdType.MESH
EPSILON = 1e-05
MASKED = -1e30
OUT, KEY, QUERY, VALUE = 0, 1, 2, 3
N_REMOTE = 120
N_LOCAL = 20


def mm(a, b):
    return jnp.dot(a, b, preferred_element_type=F32)


def kernel(
    frames, memory, lengths, gain, w_query, w_key, w_value, w_out, grad_frames, grad_memory,
    fo_v, mo_v, vg_v,
    W, WO2, fin, mem, gmem, E, U, L, X, XT, bias, K, Q, V, PT, GA, GV, ATT, PP, PPR,
    G, RA1, RA2A, RA2B, SA, RS, RF, RZ, ZQ, OB, gain_v,
    send_sem, recv_sem, local_sem, token_sem,
):
    seg = lax.axis_index("seg")
    fsdp = lax.axis_index("fsdp")
    core = lax.rem(seg, 2)
    z = lax.div(seg, 2)
    x = lax.rem(fsdp, 4)
    y = lax.div(fsdp, 4)
    other = 1 - core
    quad = lax.div(z, 4)
    place = lax.rem(z, 4)

    def wrap(a, by, n=4):
        return lax.rem(a + by + n, n)

    def device(dx=0, dy=0, dz=0, flip=False, quad_by=None):
        c = other if flip else core
        if quad_by is None:
            zz = wrap(z, dz, 16)
        else:
            zz = quad * 4 + wrap(place, quad_by)
        return (zz * 2 + c, wrap(y, dy) * 4 + wrap(x, dx))

    counter = [0]

    def remote(src, dst, to):
        i = counter[0]
        counter[0] += 1
        copy = pltpu.make_async_remote_copy(
            src_ref=src, dst_ref=dst, send_sem=send_sem.at[i], recv_sem=recv_sem.at[i],
            device_id=to, device_id_type=MESH,
        )
        copy.start()
        sent.append(copy)
        return copy

    sent = []
    lcounter = [0]

    def local(src, dst):
        i = lcounter[0]
        lcounter[0] += 1
        copy = pltpu.make_async_copy(src, dst, local_sem.at[i])
        copy.start()
        return copy

    weights = (w_out, w_key, w_query, w_value)
    own_columns = pl.ds(pl.multiple_of(core * 512, 512), 512)
    own = []
    for m in range(4):
        own.append([
            local(weights[m].at[pl.ds(32 * d, 32), own_columns], W.at[m, y, x, d])
            for d in range(2)
        ])
    in_frames = local(frames, fin)
    in_gain = local(gain, gain_v)
    in_mem = local(memory, mem)
    in_gmem = local(grad_memory, gmem)
    in_grad = [local(grad_frames.at[:, pl.ds(512 * h, 512)], U.at[core, h, pl.ds(0, 128)])
               for h in range(2)]

    partners = [device(dx=1), device(dx=-1), device(dy=1), device(dy=-1), device(flip=True),
                device(dz=1), device(dz=-1)]
    barrier = pltpu.get_barrier_semaphore()
    for partner in partners:
        pl.semaphore_signal(barrier, inc=1, device_id=partner, device_id_type=MESH)
    pl.semaphore_wait(barrier, len(partners))

    def pass_word(r):
        for i, s in enumerate((1, -1)):
            if r > 0:
                pl.semaphore_wait(token_sem.at[r - 1, i], 1)
            if r < 4:
                pl.semaphore_signal(token_sem.at[r, i], inc=1, device_id=device(dz=s),
                                    device_id_type=MESH)

    def first_to(d, s):
        return device(dx=s) if d == 0 else device(dy=s)

    def second_to(d, s):
        return device(dy=s) if d == 0 else device(dx=s)

    def ring_one(m):
        return {(d, s): remote(W.at[m, y, x, d], W.at[m, y, x, d], first_to(d, s))
                for s in (1, -1) for d in (0, 1)}

    def relay_one(m, came):
        out = {}
        for s in (1, -1):
            for d in (0, 1):
                came[d, s].wait_recv()
                rows = pl.ds(0 if s == 1 else 16, 16)
                ref = (W.at[m, y, wrap(x, -s), 0, rows] if d == 0
                       else W.at[m, wrap(y, -s), x, 1, rows])
                out[d, s] = remote(ref, ref, first_to(d, s))
        return out

    def ring_two(m, came):
        out = {}
        for d in (0, 1):
            for s in (1, -1):
                came[d, s].wait_recv()
        for s in (1, -1):
            for d in (0, 1):
                ref = W.at[m, y, :, 0] if d == 0 else W.at[m, :, x, 1]
                out[d, s] = remote(ref, ref, second_to(d, s))
        return out

    def relay_two(m, came):
        out = {}
        for s in (1, -1):
            for d in (0, 1):
                came[d, s].wait_recv()
                half = pl.ds(0 if s == 1 else 2, 2)
                ref = (W.at[m, wrap(y, -s), half, 0] if d == 0
                       else W.at[m, half, wrap(x, -s), 1])
                out[d, s] = remote(ref, ref, second_to(d, s))
        return out

    def finish(came):
        for s in (1, -1):
            for d in (0, 1):
                came[d, s].wait_recv()

    def weight(m):
        return W[m].reshape(1024, 512)

    one, one_relayed, two, two_relayed = {}, {}, {}, {}

    def begin(m):
        for copy in own[m]:
            copy.wait()
        one[m] = ring_one(m)

    for m in (OUT, KEY, QUERY):
        begin(m)

    in_frames.wait()
    in_gain.wait()
    in_mem.wait()
    sums = []
    for t in range(8):
        rows = fin[16 * t:16 * t + 16, :].astype(F32)
        centred = rows - jnp.mean(rows, axis=-1, keepdims=True)
        var = jnp.mean(centred * centred, axis=-1, keepdims=True)
        normed = (centred * lax.rsqrt(var + EPSILON) * gain_v[...]).astype(BF16)
        E[core, 16 * t:16 * t + 16, :] = normed
        sums.append(jnp.mean(normed.astype(F32), axis=0, keepdims=True))
    zeros8 = jnp.zeros((8, 1024), F32)
    E[core, 128:144, :] = jnp.concatenate(sums + [zeros8], axis=0).astype(BF16)
    E[core, 144:160, :] = jnp.concatenate([mem[...].astype(F32), zeros8], axis=0).astype(BF16)
    rows_over = remote(E.at[core], E.at[core], device(flip=True))

    for m in (OUT, KEY, QUERY):
        one_relayed[m] = relay_one(m, one[m])

    in_gmem.wait()
    for h in range(2):
        in_grad[h].wait()
        U[core, h, 128:144, :] = jnp.concatenate(
            [gmem[:, 512 * h:512 * h + 512].astype(F32), zeros8[:, :512]], axis=0).astype(BF16)
    grads_over = remote(U.at[core], U.at[core], device(flip=True))

    two[OUT] = ring_two(OUT, one_relayed[OUT])
    two[KEY] = ring_two(KEY, one_relayed[KEY])
    rows_over.wait_recv()
    tail_over = remote(E.at[1, 112:128], L.at[0], device(dz=1))
    bank_over = remote(E.at[1, 144:160], L.at[1], device(dz=1))

    slot = lax.broadcasted_iota(jnp.int32, (160, 144), 0)
    column = lax.broadcasted_iota(jnp.int32, (160, 144), 1)
    query_at = jnp.where(column < 128, column // 16, column - 128)
    key_at = jnp.where(slot < 144, slot // 16 - 1, slot - 152)
    reach = jnp.where(slot < 144, 1, 8)
    newest = jnp.where(slot < 144, 0, 1)
    back = query_at - key_at
    for g in range(2):
        base = (2 * z + g) * 8
        valid = (back >= newest) & (back <= reach) & (key_at + base >= 0)
        bias[g] = jnp.where(valid, 0.0, MASKED).astype(F32)

    X[0, 16:144, :] = E[0, 0:128, :]
    X[1, 16:144, :] = E[1, 0:128, :]
    X[1, 0:16, :] = E[0, 112:128, :]
    bank0 = E[0, 144:160, :].astype(F32)[:8]
    bank1 = E[1, 144:160, :].astype(F32)[:8]
    X[1, 144:160, :] = jnp.concatenate([bank0, bank1], axis=0).astype(BF16)

    two_relayed[OUT] = relay_two(OUT, two[OUT])
    two[QUERY] = ring_two(QUERY, one_relayed[QUERY])
    begin(VALUE)

    tail_over.wait_recv()
    bank_over.wait_recv()
    X[0, 0:16, :] = L[0]
    X[0, 144:160, :] = jnp.concatenate([L[1].astype(F32)[:8], bank0], axis=0).astype(BF16)
    for k in range(4):
        block = X[:, :, 256 * k:256 * k + 256].reshape(320, 256).astype(F32)
        block = jnp.concatenate([block, jnp.zeros((64, 256), F32)], axis=0).T.astype(BF16)
        for i in range(4):
            XT[0, k, i] = block[64 * i:64 * i + 32]
            XT[1, i, k] = block[64 * i + 32:64 * i + 64]

    finish(two_relayed[OUT])
    pass_word(0)
    out_over = remote(W.at[OUT, pl.ds(2 * other, 2)], WO2.at[core], device(flip=True))
    out_here = local(W.at[OUT, pl.ds(2 * core, 2)], WO2.at[core])
    two_relayed[KEY] = relay_two(KEY, two[KEY])
    one_relayed[VALUE] = relay_one(VALUE, one[VALUE])
    pass_word(1)

    def live_of(g, shape):
        r = lax.broadcasted_iota(jnp.int32, shape, 0)
        at = jnp.where(r < 128, r // 16, r - 128)
        return jnp.where((2 * z + g) * 8 + at < lengths[0], 1.0, 0.0).astype(F32)

    grads_over.wait_recv()
    out_here.wait()
    out_over.wait_recv()
    for g in range(2):
        ga = jnp.zeros((144, 512), F32)
        for h in range(2):
            w = WO2[h].reshape(512, 512)
            ga = ga + lax.dot_general(
                U[g, h], w, (((1,), (1,)), ((), ())), preferred_element_type=F32)
        ga = (ga * live_of(g, (144, 1))).astype(BF16)
        for p in range(4):
            GA[g, p] = ga[:, 128 * p:128 * p + 128]
    pass_word(2)

    low = lax.broadcasted_iota(jnp.int32, (1, 128), 1) < 64

    def split_heads(dst, value, g, p):
        dst[g, p, 0:160, :] = jnp.where(low, value, 0.0).astype(BF16)
        dst[g, p, 160:320, :] = jnp.where(low, 0.0, value).astype(BF16)

    def project_keys(m, dst):
        rows = X[...].reshape(320, 1024)
        for n in range(2):
            w = W[m, :, :, :, :, 256 * n:256 * n + 256].reshape(1024, 256)
            out = mm(rows, w)
            for g in range(2):
                for p in range(2):
                    split_heads(dst, out[160 * g:160 * g + 160, 128 * p:128 * p + 128], g, 2 * n + p)

    two_relayed[QUERY] = relay_two(QUERY, two[QUERY])
    finish(two_relayed[KEY])
    project_keys(KEY, K)
    pass_word(3)
    two[VALUE] = ring_two(VALUE, one_relayed[VALUE])
    finish(two_relayed[QUERY])
    query_rows = E[:, 0:144, :].reshape(288, 1024)
    for n in range(2):
        w = W[QUERY, :, :, :, :, 256 * n:256 * n + 256].reshape(1024, 256)
        out = mm(query_rows, w).astype(BF16)
        for g in range(2):
            for p in range(2):
                Q[g, 2 * n + p] = out[144 * g:144 * g + 144, 128 * p:128 * p + 128]

    def attend(i, carry):
        g = lax.div(i, 4)
        p = lax.rem(i, 4)
        scores = lax.dot_general(
            K[g, p], Q[g, p], (((1,), (1,)), ((), ())), preferred_element_type=F32)
        for h in range(2):
            s = scores[160 * h:160 * h + 160] * 0.125 + bias[g]
            e = jnp.exp(s - jnp.max(s, axis=0, keepdims=True))
            total = jnp.sum(e, axis=0, keepdims=True)
            PT[g, p, 160 * h:160 * h + 160, :] = (e / total).astype(BF16)
        return carry

    lax.fori_loop(0, 8, attend, 0)

    pass_word(4)
    for g in range(2):
        for p in range(4):
            both = mm(PT[g, p], GA[g, p])
            GV[160 * g:160 * g + 160, 128 * p:128 * p + 128] = jnp.where(
                low, both[0:160], both[160:320]).astype(BF16)
    GV[320:384, :] = jnp.zeros((64, 512), BF16)

    def a_to(d, s):
        return device(dy=s) if d == 0 else device(dx=s)

    a_at = (y, x)
    b_at = (x, y)
    ways = [(d, s) for s in (1, -1) for d in (0, 1)]
    half_of = {1: 0, -1: 1}

    def g_part(d, by, h):
        return (d, wrap(a_at[d], by), pl.ds(2 * h, 2))

    a1, a2a, a2b = {}, {}, {}
    for by in (2, 1, -1, 0):
        rows = jnp.concatenate(
            [XT[d, wrap(a_at[d], by)].reshape(128, 384) for d in range(2)], axis=0)
        block = mm(rows, GV[...]).astype(BF16)
        for d in range(2):
            G[d, wrap(a_at[d], by)] = block[128 * d:128 * d + 128].reshape(4, 32, 512)
        if by == 2:
            for d, s in ways:
                h = half_of[s]
                a1[d, s] = remote(G.at[g_part(d, 2, h)], RA1.at[d, h], a_to(d, s))
        elif by != 0:
            for d in range(2):
                h = half_of[by]
                a2b[d, by] = remote(G.at[g_part(d, by, 1 - h)], RA2B.at[d, h], a_to(d, by))
    for d, s in ways:
        h = half_of[s]
        a1[d, s].wait_recv()
        SA[d, h] = (G[g_part(d, s, h)].astype(F32) + RA1[d, h].astype(F32)).astype(BF16)
        a2a[d, s] = remote(SA.at[d, h], RA2A.at[d, h], a_to(d, s))

    two_relayed[VALUE] = relay_two(VALUE, two[VALUE])

    for d in range(2):
        for s in (1, -1):
            a2a[d, s].wait_recv()
            a2b[d, s].wait_recv()
        for h in range(2):
            total = (G[g_part(d, 0, h)].astype(F32) + RA2A[d, h].astype(F32)
                     + RA2B[d, 1 - h].astype(F32))
            RF[d, 2 * h:2 * h + 2] = total.reshape(2, 2, 16, 512)
            RS[d, 2 * h:2 * h + 2] = total.astype(BF16).reshape(2, 2, 16, 512)

    z1 = []
    for k in (2, 1, 3, 0):
        to_place = wrap(place, k)
        d = lax.div(to_place, 2)
        for o in (2, 1, 3, 0):
            if o == 0 and k == 0:
                continue
            along = x + d * (y - x)
            to_x = wrap(x, (1 - d) * o)
            to_y = wrap(y, d * o)
            to = ((quad * 4 + to_place) * 2 + core, to_y * 4 + to_x)
            z1.append(remote(RS.at[d, wrap(along, o), lax.rem(to_place, 2)], RZ.at[o, k], to))

    finish(two_relayed[VALUE])
    project_keys(VALUE, V)

    for copy in z1:
        copy.wait_recv()
    own_d = lax.div(place, 2)
    part = RF[own_d, x + own_d * (y - x), lax.rem(place, 2)]
    for o in range(4):
        for k in range(4):
            if o or k:
                part = part + RZ[o, k].astype(F32)
    ZQ[quad] = part.astype(BF16)
    z2 = {s: remote(ZQ.at[quad], ZQ.at[quad], device(dz=4 * s)) for s in (1, -1)}

    def attended(i, carry):
        g = lax.div(i, 4)
        p = lax.rem(i, 4)
        ATT[g, p] = lax.dot_general(
            PT[g, p], V[g, p], (((0,), (0,)), ((), ())), preferred_element_type=F32).astype(BF16)
        return carry

    lax.fori_loop(0, 8, attended, 0)

    z3 = {}
    for s in (1, -1):
        z2[s].wait_recv()
        cols = pl.ds(256 * half_of[s], 256)
        ref = ZQ.at[wrap(quad, -s), :, cols]
        z3[s] = remote(ref, ref, device(dz=4 * s))

    def project(g, h):
        rows = jnp.concatenate([ATT[g, p] for p in range(4)], axis=1)
        return mm(rows, WO2[h].reshape(512, 512))

    for h in range(2):
        PP[h] = project(other, h).astype(BF16)
    projected_over = remote(PP, PPR, device(flip=True))

    for s in (1, -1):
        z3[s].wait_recv()
    done = ((ZQ[0].astype(F32) + ZQ[1].astype(F32)) + ZQ[2].astype(F32)) + ZQ[3].astype(F32)
    OB[core, place] = done.astype(BF16)
    mine = OB.at[core, place]
    z4 = [remote(mine, mine, device(quad_by=k)) for k in (1, 2, 3)]
    z4 += [remote(mine, mine, device(quad_by=k, flip=True)) for k in (0, 1, 2, 3)]

    projected_over.wait_recv()
    live = live_of(core, (144, 1))
    for h in range(2):
        cols = slice(512 * h, 512 * h + 512)
        out = (project(core, h) + PPR[h].astype(F32)) * live
        fo_v[:, cols] = (fin[:, cols].astype(F32) + out[0:128]).astype(BF16)
        mo_v[:, cols] = out[128:136].astype(BF16)

    for copy in z4:
        copy.wait_recv()
    for h in range(2):
        vg_v[:, 512 * h:512 * h + 512] = OB[h].astype(F32).reshape(64, 512)
    for copy in sent:
        copy.wait_send()


def hand_out(fo_v, mo_v, vg_v, frames_out, memory_out, value_grad, sem):
    copies = [
        pltpu.make_async_copy(fo_v, frames_out, sem.at[0]),
        pltpu.make_async_copy(mo_v, memory_out, sem.at[1]),
        pltpu.make_async_copy(vg_v, value_grad, sem.at[2]),
    ]
    for copy in copies:
        copy.start()
    for copy in copies:
        copy.wait()


def on_device(
    frames, memory_in, lengths, ln_gain, w_query, w_key, w_value, w_out, grad_frames, grad_memory
):
    hbm = pl.BlockSpec(memory_space=pltpu.HBM)
    place = functools.partial(pltpu.with_memory_space_constraint, memory_space=pltpu.HBM)
    any_spec = pl.BlockSpec(memory_space=pl.ANY)
    vmem = pltpu.VMEM
    scratch = [
        vmem((4, 4, 4, 2, 32, 512), BF16),
        vmem((2, 2, 4, 2, 32, 512), BF16),
        vmem((128, 1024), BF16),
        vmem((8, 1024), BF16),
        vmem((8, 1024), BF16),
        vmem((2, 160, 1024), BF16),
        vmem((2, 2, 144, 512), BF16),
        vmem((2, 16, 1024), BF16),
        vmem((2, 160, 1024), BF16),
        vmem((2, 4, 4, 32, 384), BF16),
        vmem((2, 160, 144), F32),
        vmem((2, 4, 320, 128), BF16),
        vmem((2, 4, 144, 128), BF16),
        vmem((2, 4, 320, 128), BF16),
        vmem((2, 4, 320, 144), BF16),
        vmem((2, 4, 144, 128), BF16),
        vmem((384, 512), BF16),
        vmem((2, 4, 144, 128), BF16),
        vmem((2, 144, 512), BF16),
        vmem((2, 144, 512), BF16),
        vmem((2, 4, 4, 32, 512), BF16),
        vmem((2, 2, 2, 32, 512), BF16),
        vmem((2, 2, 2, 32, 512), BF16),
        vmem((2, 2, 2, 32, 512), BF16),
        vmem((2, 2, 2, 32, 512), BF16),
        vmem((2, 4, 2, 16, 512), BF16),
        vmem((2, 4, 2, 16, 512), F32),
        vmem((4, 4, 16, 512), BF16),
        vmem((4, 16, 512), BF16),
        vmem((2, 4, 16, 512), BF16),
        vmem((1, 1024), F32),
        pltpu.SemaphoreType.DMA((N_REMOTE,)),
        pltpu.SemaphoreType.DMA((N_REMOTE,)),
        pltpu.SemaphoreType.DMA((N_LOCAL,)),
        pltpu.SemaphoreType.REGULAR((4, 2)),
    ]
    shapes = (
        jax.ShapeDtypeStruct((128, 1024), BF16),
        jax.ShapeDtypeStruct((8, 1024), BF16),
        jax.ShapeDtypeStruct((64, 1024), F32),
    )
    results = pl.pallas_call(
        kernel,
        out_shape=shapes,
        in_specs=[hbm, hbm, pl.BlockSpec(memory_space=pltpu.SMEM)] + [hbm] * 7,
        out_specs=(pl.BlockSpec(memory_space=vmem),) * 3,
        scratch_shapes=scratch,
        compiler_params=pltpu.CompilerParams(
            collective_id=0, has_side_effects=True, vmem_limit_bytes=40 * 1024 * 1024
        ),
    )(
        place(frames.reshape(128, 1024)), place(memory_in.reshape(8, 1024)), lengths,
        place(ln_gain.reshape(1, 1024)), place(w_query), place(w_key), place(w_value),
        place(w_out), place(grad_frames.reshape(128, 1024)), place(grad_memory.reshape(8, 1024)),
    )
    frames_out, memory_out, value_grad = pl.pallas_call(
        hand_out,
        out_shape=shapes,
        in_specs=[any_spec] * 3,
        out_specs=(any_spec,) * 3,
        scratch_shapes=[pltpu.SemaphoreType.DMA((3,))],
        compiler_params=pltpu.CompilerParams(vmem_limit_bytes=1024 * 1024),
    )(*results)
    return (frames_out.reshape(frames.shape), memory_out.reshape(memory_in.shape), value_grad)


def solution(mesh):
    return jax.shard_map(
        on_device,
        mesh=mesh,
        in_specs=(
            P("fsdp", "seg", None, None),
            P("fsdp", "seg", None),
            P("fsdp"),
            P(),
            P("fsdp", None),
            P("fsdp", None),
            P("fsdp", None),
            P("fsdp", None),
            P("fsdp", "seg", None, None),
            P("fsdp", "seg", None),
        ),
        out_specs=(P("fsdp", "seg", None, None), P("fsdp", "seg", None), P("fsdp", None)),
        check_vma=False,
    )
```

```python
import functools

import jax
import jax.numpy as jnp
from jax import lax
from jax.experimental import pallas as pl
from jax.experimental.pallas import tpu as pltpu
from jax.sharding import PartitionSpec as P

F32 = jnp.float32
BF16 = jnp.bfloat16
MESH = pl.DeviceIdType.MESH
EPSILON = 1e-05
MASKED = -1e30
OUT, KEY, QUERY, VALUE = 0, 1, 2, 3
N_REMOTE = 192
N_LOCAL = 20


def mm(a, b):
    return jnp.dot(a, b, preferred_element_type=F32)


def kernel(
    frames, memory, lengths, gain, w_query, w_key, w_value, w_out, grad_frames, grad_memory,
    fo_v, mo_v, vg_v,
    W, WO2, fin, mem, gmem, E, U, L, X, XT, bias, K, Q, V, PT, GA, GV, ATT, PP, PPR,
    G, RA1, RA2A, RA2B, SA, RS, RF, RZ, ZQ, OB, gain_v,
    send_sem, recv_sem, local_sem, token_sem,
):
    seg = lax.axis_index("seg")
    fsdp = lax.axis_index("fsdp")
    core = lax.rem(seg, 2)
    z = lax.div(seg, 2)
    x = lax.rem(fsdp, 4)
    y = lax.div(fsdp, 4)
    other = 1 - core
    quad = lax.div(z, 4)
    place = lax.rem(z, 4)

    def wrap(a, by, n=4):
        return lax.rem(a + by + n, n)

    def device(dx=0, dy=0, dz=0, flip=False, quad_by=None):
        c = other if flip else core
        if quad_by is None:
            zz = wrap(z, dz, 16)
        else:
            zz = quad * 4 + wrap(place, quad_by)
        return (zz * 2 + c, wrap(y, dy) * 4 + wrap(x, dx))

    counter = [0]

    def remote(src, dst, to):
        i = counter[0]
        counter[0] += 1
        copy = pltpu.make_async_remote_copy(
            src_ref=src, dst_ref=dst, send_sem=send_sem.at[i], recv_sem=recv_sem.at[i],
            device_id=to, device_id_type=MESH,
        )
        copy.start()
        sent.append(copy)
        return copy

    sent = []
    lcounter = [0]

    def local(src, dst):
        i = lcounter[0]
        lcounter[0] += 1
        copy = pltpu.make_async_copy(src, dst, local_sem.at[i])
        copy.start()
        return copy

    weights = (w_out, w_key, w_query, w_value)
    own_columns = pl.ds(pl.multiple_of(core * 512, 512), 512)
    own = []
    for m in range(4):
        own.append([
            local(weights[m].at[pl.ds(32 * d, 32), own_columns], W.at[m, y, x, d])
            for d in range(2)
        ])
    in_frames = local(frames, fin)
    in_gain = local(gain, gain_v)
    in_mem = local(memory, mem)
    in_gmem = local(grad_memory, gmem)
    in_grad = [local(grad_frames.at[:, pl.ds(512 * h, 512)], U.at[core, h, pl.ds(0, 128)])
               for h in range(2)]

    partners = [device(dx=1), device(dx=-1), device(dy=1), device(dy=-1), device(flip=True),
                device(dz=1), device(dz=-1)]
    barrier = pltpu.get_barrier_semaphore()
    for partner in partners:
        pl.semaphore_signal(barrier, inc=1, device_id=partner, device_id_type=MESH)
    pl.semaphore_wait(barrier, len(partners))

    def pass_word(r):
        for i, s in enumerate((1, -1)):
            if r > 0:
                pl.semaphore_wait(token_sem.at[r - 1, i], 1)
            if r < 4:
                pl.semaphore_signal(token_sem.at[r, i], inc=1, device_id=device(dz=s),
                                    device_id_type=MESH)

    def first_to(d, s):
        return device(dx=s) if d == 0 else device(dy=s)

    def second_to(d, s):
        return device(dy=s) if d == 0 else device(dx=s)

    def piece(m, d, first=0, second=0, rows=None):
        dx, dy = (first, second) if d == 0 else (second, first)
        at = (m, wrap(y, dy), wrap(x, dx), d)
        return W.at[at if rows is None else at + (rows,)]

    flows = [(d, s) for s in (1, -1) for d in (0, 1)]
    direct, halves, forwarded, relayed = {}, {}, {}, {}

    def forward(m, d, kind):
        for s in (1, -1):
            ref = piece(m, d, first=kind)
            forwarded[m, d, s, kind] = remote(ref, ref, second_to(d, s))

    def stage0(m):
        for copy in own[m]:
            copy.wait()
        for d, s in flows:
            ref = piece(m, d)
            direct[m, d, s] = remote(ref, ref, first_to(d, s))
        for d in (0, 1):
            forward(m, d, 0)

    def stage1(m):
        for d, s in flows:
            direct[m, d, s].wait_recv()
            ref = piece(m, d, first=-s, rows=pl.ds(0 if s == 1 else 16, 16))
            halves[m, d, s] = remote(ref, ref, first_to(d, s))
        for d, s in flows:
            forward(m, d, -s)

    def stage2(m):
        for d in (0, 1):
            for s in (1, -1):
                halves[m, d, s].wait_recv()
            forward(m, d, 2)

    def stage3(m, kinds=(0, 1)):
        for i in kinds:
            for d, s in flows:
                kind = ((0, -1), (1, 2))[(1 - s) // 2][i]
                forwarded[m, d, s, kind].wait_recv()
                ref = piece(m, d, first=kind, second=-s)
                relayed[m, d, s, kind] = remote(ref, ref, second_to(d, s))

    def stage4(m):
        for d, s in flows:
            for kind in ((1, 2), (0, -1))[(1 - s) // 2]:
                forwarded[m, d, s, kind].wait_recv()
        for d, s in flows:
            for kind in ((0, -1), (1, 2))[(1 - s) // 2]:
                relayed[m, d, s, kind].wait_recv()

    for m in (OUT, KEY, QUERY):
        stage0(m)

    in_frames.wait()
    in_gain.wait()
    in_mem.wait()
    sums = []
    for t in range(8):
        rows = fin[16 * t:16 * t + 16, :].astype(F32)
        centred = rows - jnp.mean(rows, axis=-1, keepdims=True)
        var = jnp.mean(centred * centred, axis=-1, keepdims=True)
        normed = (centred * lax.rsqrt(var + EPSILON) * gain_v[...]).astype(BF16)
        E[core, 16 * t:16 * t + 16, :] = normed
        sums.append(jnp.mean(normed.astype(F32), axis=0, keepdims=True))
    zeros8 = jnp.zeros((8, 1024), F32)
    E[core, 128:144, :] = jnp.concatenate(sums + [zeros8], axis=0).astype(BF16)
    E[core, 144:160, :] = jnp.concatenate([mem[...].astype(F32), zeros8], axis=0).astype(BF16)
    rows_over = remote(E.at[core], E.at[core], device(flip=True))

    for m in (OUT, KEY, QUERY):
        stage1(m)

    in_gmem.wait()
    for h in range(2):
        in_grad[h].wait()
        U[core, h, 128:144, :] = jnp.concatenate(
            [gmem[:, 512 * h:512 * h + 512].astype(F32), zeros8[:, :512]], axis=0).astype(BF16)
    grads_over = remote(U.at[core], U.at[core], device(flip=True))

    stage2(OUT)
    stage2(KEY)
    rows_over.wait_recv()
    tail_over = remote(E.at[1, 112:128], L.at[0], device(dz=1))
    bank_over = remote(E.at[1, 144:160], L.at[1], device(dz=1))

    slot = lax.broadcasted_iota(jnp.int32, (160, 144), 0)
    column = lax.broadcasted_iota(jnp.int32, (160, 144), 1)
    query_at = jnp.where(column < 128, column // 16, column - 128)
    key_at = jnp.where(slot < 144, slot // 16 - 1, slot - 152)
    reach = jnp.where(slot < 144, 1, 8)
    newest = jnp.where(slot < 144, 0, 1)
    back = query_at - key_at
    for g in range(2):
        base = (2 * z + g) * 8
        valid = (back >= newest) & (back <= reach) & (key_at + base >= 0)
        bias[g] = jnp.where(valid, 0.0, MASKED).astype(F32)

    X[0, 16:144, :] = E[0, 0:128, :]
    X[1, 16:144, :] = E[1, 0:128, :]
    X[1, 0:16, :] = E[0, 112:128, :]
    bank0 = E[0, 144:160, :].astype(F32)[:8]
    bank1 = E[1, 144:160, :].astype(F32)[:8]
    X[1, 144:160, :] = jnp.concatenate([bank0, bank1], axis=0).astype(BF16)

    stage3(OUT)
    stage2(QUERY)
    stage3(KEY)

    tail_over.wait_recv()
    bank_over.wait_recv()
    X[0, 0:16, :] = L[0]
    X[0, 144:160, :] = jnp.concatenate([L[1].astype(F32)[:8], bank0], axis=0).astype(BF16)
    for k in range(4):
        block = X[:, :, 256 * k:256 * k + 256].reshape(320, 256).astype(F32)
        block = jnp.concatenate([block, jnp.zeros((64, 256), F32)], axis=0).T.astype(BF16)
        for i in range(4):
            XT[0, k, i] = block[64 * i:64 * i + 32]
            XT[1, i, k] = block[64 * i + 32:64 * i + 64]

    stage4(OUT)
    pass_word(0)
    out_over = remote(W.at[OUT, pl.ds(2 * other, 2)], WO2.at[core], device(flip=True))
    out_here = local(W.at[OUT, pl.ds(2 * core, 2)], WO2.at[core])
    stage3(QUERY)
    stage0(VALUE)
    pass_word(1)

    def live_of(g, shape):
        r = lax.broadcasted_iota(jnp.int32, shape, 0)
        at = jnp.where(r < 128, r // 16, r - 128)
        return jnp.where((2 * z + g) * 8 + at < lengths[0], 1.0, 0.0).astype(F32)

    low = lax.broadcasted_iota(jnp.int32, (1, 128), 1) < 64

    def split_heads(dst, value, g, p):
        dst[g, p, 0:160, :] = jnp.where(low, value, 0.0).astype(BF16)
        dst[g, p, 160:320, :] = jnp.where(low, 0.0, value).astype(BF16)

    def project_keys(m, dst):
        rows = X[...].reshape(320, 1024)
        for n in range(2):
            w = W[m, :, :, :, :, 256 * n:256 * n + 256].reshape(1024, 256)
            out = mm(rows, w)
            for g in range(2):
                for p in range(2):
                    split_heads(dst, out[160 * g:160 * g + 160, 128 * p:128 * p + 128], g, 2 * n + p)

    stage4(KEY)
    project_keys(KEY, K)
    pass_word(2)
    stage1(VALUE)
    stage4(QUERY)
    query_rows = E[:, 0:144, :].reshape(288, 1024)
    for n in range(2):
        w = W[QUERY, :, :, :, :, 256 * n:256 * n + 256].reshape(1024, 256)
        out = mm(query_rows, w).astype(BF16)
        for g in range(2):
            for p in range(2):
                Q[g, 2 * n + p] = out[144 * g:144 * g + 144, 128 * p:128 * p + 128]

    def attend(i, carry):
        g = lax.div(i, 4)
        p = lax.rem(i, 4)
        scores = lax.dot_general(
            K[g, p], Q[g, p], (((1,), (1,)), ((), ())), preferred_element_type=F32)
        for h in range(2):
            s = scores[160 * h:160 * h + 160] * 0.125 + bias[g]
            e = jnp.exp(s - jnp.max(s, axis=0, keepdims=True))
            total = jnp.sum(e, axis=0, keepdims=True)
            PT[g, p, 160 * h:160 * h + 160, :] = (e / total).astype(BF16)
        return carry

    lax.fori_loop(0, 8, attend, 0)

    pass_word(3)
    stage2(VALUE)
    grads_over.wait_recv()
    out_here.wait()
    out_over.wait_recv()
    for g in range(2):
        ga = jnp.zeros((144, 512), F32)
        for h in range(2):
            w = WO2[h].reshape(512, 512)
            ga = ga + lax.dot_general(
                U[g, h], w, (((1,), (1,)), ((), ())), preferred_element_type=F32)
        ga = (ga * live_of(g, (144, 1))).astype(BF16)
        for p in range(4):
            GA[g, p] = ga[:, 128 * p:128 * p + 128]
    pass_word(4)
    for g in range(2):
        for p in range(4):
            both = mm(PT[g, p], GA[g, p])
            GV[160 * g:160 * g + 160, 128 * p:128 * p + 128] = jnp.where(
                low, both[0:160], both[160:320]).astype(BF16)
    GV[320:384, :] = jnp.zeros((64, 512), BF16)

    def a_to(d, s):
        return device(dy=s) if d == 0 else device(dx=s)

    a_at = (y, x)
    b_at = (x, y)
    ways = [(d, s) for s in (1, -1) for d in (0, 1)]
    half_of = {1: 0, -1: 1}

    def g_part(d, by, h):
        return (d, wrap(a_at[d], by), pl.ds(2 * h, 2))

    a1, a2a, a2b = {}, {}, {}
    for by in (2, 1, -1, 0):
        rows = jnp.concatenate(
            [XT[d, wrap(a_at[d], by)].reshape(128, 384) for d in range(2)], axis=0)
        block = mm(rows, GV[...]).astype(BF16)
        for d in range(2):
            G[d, wrap(a_at[d], by)] = block[128 * d:128 * d + 128].reshape(4, 32, 512)
        if by == 2:
            for d, s in ways:
                h = half_of[s]
                a1[d, s] = remote(G.at[g_part(d, 2, h)], RA1.at[d, h], a_to(d, s))
        elif by != 0:
            for d in range(2):
                h = half_of[by]
                a2b[d, by] = remote(G.at[g_part(d, by, 1 - h)], RA2B.at[d, h], a_to(d, by))
    for d, s in ways:
        h = half_of[s]
        a1[d, s].wait_recv()
        SA[d, h] = (G[g_part(d, s, h)].astype(F32) + RA1[d, h].astype(F32)).astype(BF16)
        a2a[d, s] = remote(SA.at[d, h], RA2A.at[d, h], a_to(d, s))

    stage3(VALUE)

    for d in range(2):
        for s in (1, -1):
            a2a[d, s].wait_recv()
            a2b[d, s].wait_recv()
        for h in range(2):
            total = (G[g_part(d, 0, h)].astype(F32) + RA2A[d, h].astype(F32)
                     + RA2B[d, 1 - h].astype(F32))
            RF[d, 2 * h:2 * h + 2] = total.reshape(2, 2, 16, 512)
            RS[d, 2 * h:2 * h + 2] = total.astype(BF16).reshape(2, 2, 16, 512)

    z1 = []
    for k in (2, 1, 3, 0):
        to_place = wrap(place, k)
        d = lax.div(to_place, 2)
        for o in (2, 1, 3, 0):
            if o == 0 and k == 0:
                continue
            along = x + d * (y - x)
            to_x = wrap(x, (1 - d) * o)
            to_y = wrap(y, d * o)
            to = ((quad * 4 + to_place) * 2 + core, to_y * 4 + to_x)
            z1.append(remote(RS.at[d, wrap(along, o), lax.rem(to_place, 2)], RZ.at[o, k], to))

    stage4(VALUE)
    project_keys(VALUE, V)

    for copy in z1:
        copy.wait_recv()
    own_d = lax.div(place, 2)
    part = RF[own_d, x + own_d * (y - x), lax.rem(place, 2)]
    for o in range(4):
        for k in range(4):
            if o or k:
                part = part + RZ[o, k].astype(F32)
    ZQ[quad] = part.astype(BF16)
    z2 = {s: remote(ZQ.at[quad], ZQ.at[quad], device(dz=4 * s)) for s in (1, -1)}

    def attended(i, carry):
        g = lax.div(i, 4)
        p = lax.rem(i, 4)
        ATT[g, p] = lax.dot_general(
            PT[g, p], V[g, p], (((0,), (0,)), ((), ())), preferred_element_type=F32).astype(BF16)
        return carry

    lax.fori_loop(0, 8, attended, 0)

    z3 = {}
    for s in (1, -1):
        z2[s].wait_recv()
        cols = pl.ds(256 * half_of[s], 256)
        ref = ZQ.at[wrap(quad, -s), :, cols]
        z3[s] = remote(ref, ref, device(dz=4 * s))

    def project(g, h):
        rows = jnp.concatenate([ATT[g, p] for p in range(4)], axis=1)
        return mm(rows, WO2[h].reshape(512, 512))

    for h in range(2):
        PP[h] = project(other, h).astype(BF16)
    projected_over = remote(PP, PPR, device(flip=True))

    for s in (1, -1):
        z3[s].wait_recv()
    done = ((ZQ[0].astype(F32) + ZQ[1].astype(F32)) + ZQ[2].astype(F32)) + ZQ[3].astype(F32)
    OB[core, place] = done.astype(BF16)
    mine = OB.at[core, place]
    z4 = [remote(mine, mine, device(quad_by=k)) for k in (1, 2, 3)]
    z4 += [remote(mine, mine, device(quad_by=k, flip=True)) for k in (0, 1, 2, 3)]

    projected_over.wait_recv()
    live = live_of(core, (144, 1))
    for h in range(2):
        cols = slice(512 * h, 512 * h + 512)
        out = (project(core, h) + PPR[h].astype(F32)) * live
        fo_v[:, cols] = (fin[:, cols].astype(F32) + out[0:128]).astype(BF16)
        mo_v[:, cols] = out[128:136].astype(BF16)

    for copy in z4:
        copy.wait_recv()
    for h in range(2):
        vg_v[:, 512 * h:512 * h + 512] = OB[h].astype(F32).reshape(64, 512)
    for copy in sent:
        copy.wait_send()


def hand_out(fo_v, mo_v, vg_v, frames_out, memory_out, value_grad, sem):
    copies = [
        pltpu.make_async_copy(fo_v, frames_out, sem.at[0]),
        pltpu.make_async_copy(mo_v, memory_out, sem.at[1]),
        pltpu.make_async_copy(vg_v, value_grad, sem.at[2]),
    ]
    for copy in copies:
        copy.start()
    for copy in copies:
        copy.wait()


def on_device(
    frames, memory_in, lengths, ln_gain, w_query, w_key, w_value, w_out, grad_frames, grad_memory
):
    hbm = pl.BlockSpec(memory_space=pltpu.HBM)
    place = functools.partial(pltpu.with_memory_space_constraint, memory_space=pltpu.HBM)
    any_spec = pl.BlockSpec(memory_space=pl.ANY)
    vmem = pltpu.VMEM
    scratch = [
        vmem((4, 4, 4, 2, 32, 512), BF16),
        vmem((2, 2, 4, 2, 32, 512), BF16),
        vmem((128, 1024), BF16),
        vmem((8, 1024), BF16),
        vmem((8, 1024), BF16),
        vmem((2, 160, 1024), BF16),
        vmem((2, 2, 144, 512), BF16),
        vmem((2, 16, 1024), BF16),
        vmem((2, 160, 1024), BF16),
        vmem((2, 4, 4, 32, 384), BF16),
        vmem((2, 160, 144), F32),
        vmem((2, 4, 320, 128), BF16),
        vmem((2, 4, 144, 128), BF16),
        vmem((2, 4, 320, 128), BF16),
        vmem((2, 4, 320, 144), BF16),
        vmem((2, 4, 144, 128), BF16),
        vmem((384, 512), BF16),
        vmem((2, 4, 144, 128), BF16),
        vmem((2, 144, 512), BF16),
        vmem((2, 144, 512), BF16),
        vmem((2, 4, 4, 32, 512), BF16),
        vmem((2, 2, 2, 32, 512), BF16),
        vmem((2, 2, 2, 32, 512), BF16),
        vmem((2, 2, 2, 32, 512), BF16),
        vmem((2, 2, 2, 32, 512), BF16),
        vmem((2, 4, 2, 16, 512), BF16),
        vmem((2, 4, 2, 16, 512), F32),
        vmem((4, 4, 16, 512), BF16),
        vmem((4, 16, 512), BF16),
        vmem((2, 4, 16, 512), BF16),
        vmem((1, 1024), F32),
        pltpu.SemaphoreType.DMA((N_REMOTE,)),
        pltpu.SemaphoreType.DMA((N_REMOTE,)),
        pltpu.SemaphoreType.DMA((N_LOCAL,)),
        pltpu.SemaphoreType.REGULAR((4, 2)),
    ]
    shapes = (
        jax.ShapeDtypeStruct((128, 1024), BF16),
        jax.ShapeDtypeStruct((8, 1024), BF16),
        jax.ShapeDtypeStruct((64, 1024), F32),
    )
    results = pl.pallas_call(
        kernel,
        out_shape=shapes,
        in_specs=[hbm, hbm, pl.BlockSpec(memory_space=pltpu.SMEM)] + [hbm] * 7,
        out_specs=(pl.BlockSpec(memory_space=vmem),) * 3,
        scratch_shapes=scratch,
        compiler_params=pltpu.CompilerParams(
            collective_id=0, has_side_effects=True, vmem_limit_bytes=40 * 1024 * 1024
        ),
    )(
        place(frames.reshape(128, 1024)), place(memory_in.reshape(8, 1024)), lengths,
        place(ln_gain.reshape(1, 1024)), place(w_query), place(w_key), place(w_value),
        place(w_out), place(grad_frames.reshape(128, 1024)), place(grad_memory.reshape(8, 1024)),
    )
    frames_out, memory_out, value_grad = pl.pallas_call(
        hand_out,
        out_shape=shapes,
        in_specs=[any_spec] * 3,
        out_specs=(any_spec,) * 3,
        scratch_shapes=[pltpu.SemaphoreType.DMA((3,))],
        compiler_params=pltpu.CompilerParams(vmem_limit_bytes=1024 * 1024),
    )(*results)
    return (frames_out.reshape(frames.shape), memory_out.reshape(memory_in.shape), value_grad)


def solution(mesh):
    return jax.shard_map(
        on_device,
        mesh=mesh,
        in_specs=(
            P("fsdp", "seg", None, None),
            P("fsdp", "seg", None),
            P("fsdp"),
            P(),
            P("fsdp", None),
            P("fsdp", None),
            P("fsdp", None),
            P("fsdp", None),
            P("fsdp", "seg", None, None),
            P("fsdp", "seg", None),
        ),
        out_specs=(P("fsdp", "seg", None, None), P("fsdp", "seg", None), P("fsdp", None)),
        check_vma=False,
    )
```

```python
import functools

import jax
import jax.numpy as jnp
from jax import lax
from jax.experimental import pallas as pl
from jax.experimental.pallas import tpu as pltpu
from jax.sharding import PartitionSpec as P

F32 = jnp.float32
BF16 = jnp.bfloat16
MESH = pl.DeviceIdType.MESH
EPSILON = 1e-05
MASKED = -1e30
OUT, KEY, QUERY, VALUE = 0, 1, 2, 3
N_REMOTE = 192
N_LOCAL = 20


def mm(a, b):
    return jnp.dot(a, b, preferred_element_type=F32)


def kernel(
    frames, memory, lengths, gain, w_query, w_key, w_value, w_out, grad_frames, grad_memory,
    fo_v, mo_v, vg_v,
    W, WO2, fin, mem, gmem, E, U, L, X, XT, bias, K, Q, V, PT, GA, GV, ATT, PP, PPR,
    G, RA1, RA2A, RA2B, SA, RS, RF, RZ, ZQ, OB, gain_v,
    send_sem, recv_sem, local_sem, token_sem,
):
    seg = lax.axis_index("seg")
    fsdp = lax.axis_index("fsdp")
    core = lax.rem(seg, 2)
    z = lax.div(seg, 2)
    x = lax.rem(fsdp, 4)
    y = lax.div(fsdp, 4)
    other = 1 - core
    quad = lax.div(z, 4)
    place = lax.rem(z, 4)

    def wrap(a, by, n=4):
        return lax.rem(a + by + n, n)

    def device(dx=0, dy=0, dz=0, flip=False, quad_by=None):
        c = other if flip else core
        if quad_by is None:
            zz = wrap(z, dz, 16)
        else:
            zz = quad * 4 + wrap(place, quad_by)
        return (zz * 2 + c, wrap(y, dy) * 4 + wrap(x, dx))

    counter = [0]

    def remote(src, dst, to):
        i = counter[0]
        counter[0] += 1
        copy = pltpu.make_async_remote_copy(
            src_ref=src, dst_ref=dst, send_sem=send_sem.at[i], recv_sem=recv_sem.at[i],
            device_id=to, device_id_type=MESH,
        )
        copy.start()
        sent.append(copy)
        return copy

    sent = []
    lcounter = [0]

    def local(src, dst):
        i = lcounter[0]
        lcounter[0] += 1
        copy = pltpu.make_async_copy(src, dst, local_sem.at[i])
        copy.start()
        return copy

    weights = (w_out, w_key, w_query, w_value)
    own_columns = pl.ds(pl.multiple_of(core * 512, 512), 512)
    own = []
    for m in range(4):
        own.append([
            local(weights[m].at[pl.ds(32 * d, 32), own_columns], W.at[m, y, x, d])
            for d in range(2)
        ])
    in_frames = local(frames, fin)
    in_gain = local(gain, gain_v)
    in_mem = local(memory, mem)
    in_gmem = local(grad_memory, gmem)
    in_grad = [local(grad_frames.at[:, pl.ds(512 * h, 512)], U.at[core, h, pl.ds(0, 128)])
               for h in range(2)]

    partners = [device(dx=1), device(dx=-1), device(dy=1), device(dy=-1), device(flip=True),
                device(dz=1), device(dz=-1)]
    barrier = pltpu.get_barrier_semaphore()
    for partner in partners:
        pl.semaphore_signal(barrier, inc=1, device_id=partner, device_id_type=MESH)
    pl.semaphore_wait(barrier, len(partners))

    def pass_word(r):
        for i, s in enumerate((1, -1)):
            if r > 0:
                pl.semaphore_wait(token_sem.at[r - 1, i], 1)
            if r < 4:
                pl.semaphore_signal(token_sem.at[r, i], inc=1, device_id=device(dz=s),
                                    device_id_type=MESH)

    def first_to(d, s):
        return device(dx=s) if d == 0 else device(dy=s)

    def second_to(d, s):
        return device(dy=s) if d == 0 else device(dx=s)

    def piece(m, d, first=0, second=0, rows=None):
        dx, dy = (first, second) if d == 0 else (second, first)
        at = (m, wrap(y, dy), wrap(x, dx), d)
        return W.at[at if rows is None else at + (rows,)]

    flows = [(d, s) for s in (1, -1) for d in (0, 1)]
    direct, halves, forwarded, relayed = {}, {}, {}, {}

    def forward(m, d, kind):
        for s in (1, -1):
            ref = piece(m, d, first=kind)
            forwarded[m, d, s, kind] = remote(ref, ref, second_to(d, s))

    def stage0(m):
        for copy in own[m]:
            copy.wait()
        for d, s in flows:
            ref = piece(m, d)
            direct[m, d, s] = remote(ref, ref, first_to(d, s))
        for d in (0, 1):
            forward(m, d, 0)

    def stage1(m):
        for d, s in flows:
            direct[m, d, s].wait_recv()
            ref = piece(m, d, first=-s, rows=pl.ds(0 if s == 1 else 16, 16))
            halves[m, d, s] = remote(ref, ref, first_to(d, s))
        for d, s in flows:
            forward(m, d, -s)

    def stage2(m):
        for d in (0, 1):
            for s in (1, -1):
                halves[m, d, s].wait_recv()
            forward(m, d, 2)

    def stage3(m, kinds=(0, 1)):
        for i in kinds:
            for d, s in flows:
                kind = ((0, -1), (1, 2))[(1 - s) // 2][i]
                forwarded[m, d, s, kind].wait_recv()
                ref = piece(m, d, first=kind, second=-s)
                relayed[m, d, s, kind] = remote(ref, ref, second_to(d, s))

    def stage4(m):
        for d, s in flows:
            for kind in ((1, 2), (0, -1))[(1 - s) // 2]:
                forwarded[m, d, s, kind].wait_recv()
        for d, s in flows:
            for kind in ((0, -1), (1, 2))[(1 - s) // 2]:
                relayed[m, d, s, kind].wait_recv()

    for m in (OUT, KEY, QUERY):
        stage0(m)

    in_frames.wait()
    in_gain.wait()
    in_mem.wait()
    sums = []
    for t in range(8):
        rows = fin[16 * t:16 * t + 16, :].astype(F32)
        centred = rows - jnp.mean(rows, axis=-1, keepdims=True)
        var = jnp.mean(centred * centred, axis=-1, keepdims=True)
        normed = (centred * lax.rsqrt(var + EPSILON) * gain_v[...]).astype(BF16)
        E[core, 16 * t:16 * t + 16, :] = normed
        sums.append(jnp.mean(normed.astype(F32), axis=0, keepdims=True))
    zeros8 = jnp.zeros((8, 1024), F32)
    E[core, 128:144, :] = jnp.concatenate(sums + [zeros8], axis=0).astype(BF16)
    E[core, 144:160, :] = jnp.concatenate([mem[...].astype(F32), zeros8], axis=0).astype(BF16)
    rows_over = remote(E.at[core], E.at[core], device(flip=True))

    for m in (OUT, KEY, QUERY):
        stage1(m)

    in_gmem.wait()
    for h in range(2):
        in_grad[h].wait()
        U[core, h, 128:144, :] = jnp.concatenate(
            [gmem[:, 512 * h:512 * h + 512].astype(F32), zeros8[:, :512]], axis=0).astype(BF16)
    grads_over = remote(U.at[core], U.at[core], device(flip=True))

    stage2(OUT)
    stage2(KEY)
    rows_over.wait_recv()
    tail_over = remote(E.at[1, 112:128], L.at[0], device(dz=1))
    bank_over = remote(E.at[1, 144:160], L.at[1], device(dz=1))

    slot = lax.broadcasted_iota(jnp.int32, (160, 144), 0)
    column = lax.broadcasted_iota(jnp.int32, (160, 144), 1)
    query_at = jnp.where(column < 128, column // 16, column - 128)
    key_at = jnp.where(slot < 144, slot // 16 - 1, slot - 152)
    reach = jnp.where(slot < 144, 1, 8)
    newest = jnp.where(slot < 144, 0, 1)
    back = query_at - key_at
    for g in range(2):
        base = (2 * z + g) * 8
        valid = (back >= newest) & (back <= reach) & (key_at + base >= 0)
        bias[g] = jnp.where(valid, 0.0, MASKED).astype(F32)

    X[0, 16:144, :] = E[0, 0:128, :]
    X[1, 16:144, :] = E[1, 0:128, :]
    X[1, 0:16, :] = E[0, 112:128, :]
    bank0 = E[0, 144:160, :].astype(F32)[:8]
    bank1 = E[1, 144:160, :].astype(F32)[:8]
    X[1, 144:160, :] = jnp.concatenate([bank0, bank1], axis=0).astype(BF16)


    tail_over.wait_recv()
    bank_over.wait_recv()
    X[0, 0:16, :] = L[0]
    X[0, 144:160, :] = jnp.concatenate([L[1].astype(F32)[:8], bank0], axis=0).astype(BF16)
    for k in range(4):
        block = X[:, :, 256 * k:256 * k + 256].reshape(320, 256).astype(F32)
        block = jnp.concatenate([block, jnp.zeros((64, 256), F32)], axis=0).T.astype(BF16)
        for i in range(4):
            XT[0, k, i] = block[64 * i:64 * i + 32]
            XT[1, i, k] = block[64 * i + 32:64 * i + 64]

    stage2(QUERY)
    stage3(OUT)
    stage3(KEY)
    stage4(OUT)
    pass_word(0)
    out_over = remote(W.at[OUT, pl.ds(2 * other, 2)], WO2.at[core], device(flip=True))
    out_here = local(W.at[OUT, pl.ds(2 * core, 2)], WO2.at[core])
    stage3(QUERY)
    stage0(VALUE)
    pass_word(1)

    def live_of(g, shape):
        r = lax.broadcasted_iota(jnp.int32, shape, 0)
        at = jnp.where(r < 128, r // 16, r - 128)
        return jnp.where((2 * z + g) * 8 + at < lengths[0], 1.0, 0.0).astype(F32)

    low = lax.broadcasted_iota(jnp.int32, (1, 128), 1) < 64

    def split_heads(dst, value, g, p):
        dst[g, p, 0:160, :] = jnp.where(low, value, 0.0).astype(BF16)
        dst[g, p, 160:320, :] = jnp.where(low, 0.0, value).astype(BF16)

    def project_keys(m, dst):
        rows = X[...].reshape(320, 1024)
        for n in range(2):
            w = W[m, :, :, :, :, 256 * n:256 * n + 256].reshape(1024, 256)
            out = mm(rows, w)
            for g in range(2):
                for p in range(2):
                    split_heads(dst, out[160 * g:160 * g + 160, 128 * p:128 * p + 128], g, 2 * n + p)

    stage4(KEY)
    project_keys(KEY, K)
    pass_word(2)
    grads_over.wait_recv()
    out_here.wait()
    out_over.wait_recv()
    for g in range(2):
        ga = jnp.zeros((144, 512), F32)
        for h in range(2):
            w = WO2[h].reshape(512, 512)
            ga = ga + lax.dot_general(
                U[g, h], w, (((1,), (1,)), ((), ())), preferred_element_type=F32)
        ga = (ga * live_of(g, (144, 1))).astype(BF16)
        for p in range(4):
            GA[g, p] = ga[:, 128 * p:128 * p + 128]
    stage4(QUERY)
    query_rows = E[:, 0:144, :].reshape(288, 1024)
    for n in range(2):
        w = W[QUERY, :, :, :, :, 256 * n:256 * n + 256].reshape(1024, 256)
        out = mm(query_rows, w).astype(BF16)
        for g in range(2):
            for p in range(2):
                Q[g, 2 * n + p] = out[144 * g:144 * g + 144, 128 * p:128 * p + 128]

    stage1(VALUE)

    def attend(i, carry):
        g = lax.div(i, 4)
        p = lax.rem(i, 4)
        scores = lax.dot_general(
            K[g, p], Q[g, p], (((1,), (1,)), ((), ())), preferred_element_type=F32)
        for h in range(2):
            s = scores[160 * h:160 * h + 160] * 0.125 + bias[g]
            e = jnp.exp(s - jnp.max(s, axis=0, keepdims=True))
            total = jnp.sum(e, axis=0, keepdims=True)
            PT[g, p, 160 * h:160 * h + 160, :] = (e / total).astype(BF16)
        return carry

    lax.fori_loop(0, 8, attend, 0)

    pass_word(3)
    pass_word(4)
    for g in range(2):
        for p in range(4):
            both = mm(PT[g, p], GA[g, p])
            GV[160 * g:160 * g + 160, 128 * p:128 * p + 128] = jnp.where(
                low, both[0:160], both[160:320]).astype(BF16)
    GV[320:384, :] = jnp.zeros((64, 512), BF16)

    def a_to(d, s):
        return device(dy=s) if d == 0 else device(dx=s)

    a_at = (y, x)
    b_at = (x, y)
    ways = [(d, s) for s in (1, -1) for d in (0, 1)]
    half_of = {1: 0, -1: 1}

    def g_part(d, by, h):
        return (d, wrap(a_at[d], by), pl.ds(2 * h, 2))

    a1, a2a, a2b = {}, {}, {}
    for by in (2, 1, -1, 0):
        rows = jnp.concatenate(
            [XT[d, wrap(a_at[d], by)].reshape(128, 384) for d in range(2)], axis=0)
        block = mm(rows, GV[...]).astype(BF16)
        for d in range(2):
            G[d, wrap(a_at[d], by)] = block[128 * d:128 * d + 128].reshape(4, 32, 512)
        if by == 2:
            for d, s in ways:
                h = half_of[s]
                a1[d, s] = remote(G.at[g_part(d, 2, h)], RA1.at[d, h], a_to(d, s))
        elif by != 0:
            for d in range(2):
                h = half_of[by]
                a2b[d, by] = remote(G.at[g_part(d, by, 1 - h)], RA2B.at[d, h], a_to(d, by))
    for d, s in ways:
        h = half_of[s]
        a1[d, s].wait_recv()
        SA[d, h] = (G[g_part(d, s, h)].astype(F32) + RA1[d, h].astype(F32)).astype(BF16)
        a2a[d, s] = remote(SA.at[d, h], RA2A.at[d, h], a_to(d, s))

    stage2(VALUE)

    for d in range(2):
        for s in (1, -1):
            a2a[d, s].wait_recv()
            a2b[d, s].wait_recv()
        for h in range(2):
            total = (G[g_part(d, 0, h)].astype(F32) + RA2A[d, h].astype(F32)
                     + RA2B[d, 1 - h].astype(F32))
            RF[d, 2 * h:2 * h + 2] = total.reshape(2, 2, 16, 512)
            RS[d, 2 * h:2 * h + 2] = total.astype(BF16).reshape(2, 2, 16, 512)

    z1 = []
    for k in (2, 1, 3, 0):
        to_place = wrap(place, k)
        d = lax.div(to_place, 2)
        for o in (2, 1, 3, 0):
            if o == 0 and k == 0:
                continue
            along = x + d * (y - x)
            to_x = wrap(x, (1 - d) * o)
            to_y = wrap(y, d * o)
            to = ((quad * 4 + to_place) * 2 + core, to_y * 4 + to_x)
            z1.append(remote(RS.at[d, wrap(along, o), lax.rem(to_place, 2)], RZ.at[o, k], to))

    stage3(VALUE)

    for copy in z1:
        copy.wait_recv()
    own_d = lax.div(place, 2)
    part = RF[own_d, x + own_d * (y - x), lax.rem(place, 2)]
    for o in range(4):
        for k in range(4):
            if o or k:
                part = part + RZ[o, k].astype(F32)
    ZQ[quad] = part.astype(BF16)
    z2 = {s: remote(ZQ.at[quad], ZQ.at[quad], device(dz=4 * s)) for s in (1, -1)}

    stage4(VALUE)
    project_keys(VALUE, V)

    def attended(i, carry):
        g = lax.div(i, 4)
        p = lax.rem(i, 4)
        ATT[g, p] = lax.dot_general(
            PT[g, p], V[g, p], (((0,), (0,)), ((), ())), preferred_element_type=F32).astype(BF16)
        return carry

    lax.fori_loop(0, 8, attended, 0)

    z3 = {}
    for s in (1, -1):
        z2[s].wait_recv()
        cols = pl.ds(256 * half_of[s], 256)
        ref = ZQ.at[wrap(quad, -s), :, cols]
        z3[s] = remote(ref, ref, device(dz=4 * s))

    def project(g, h):
        rows = jnp.concatenate([ATT[g, p] for p in range(4)], axis=1)
        return mm(rows, WO2[h].reshape(512, 512))

    for h in range(2):
        PP[h] = project(other, h).astype(BF16)
    projected_over = remote(PP, PPR, device(flip=True))

    for s in (1, -1):
        z3[s].wait_recv()
    done = ((ZQ[0].astype(F32) + ZQ[1].astype(F32)) + ZQ[2].astype(F32)) + ZQ[3].astype(F32)
    OB[core, place] = done.astype(BF16)
    mine = OB.at[core, place]
    z4 = [remote(mine, mine, device(quad_by=k)) for k in (1, 2, 3)]
    z4 += [remote(mine, mine, device(quad_by=k, flip=True)) for k in (0, 1, 2, 3)]

    projected_over.wait_recv()
    live = live_of(core, (144, 1))
    for h in range(2):
        cols = slice(512 * h, 512 * h + 512)
        out = (project(core, h) + PPR[h].astype(F32)) * live
        fo_v[:, cols] = (fin[:, cols].astype(F32) + out[0:128]).astype(BF16)
        mo_v[:, cols] = out[128:136].astype(BF16)

    for copy in z4:
        copy.wait_recv()
    for h in range(2):
        vg_v[:, 512 * h:512 * h + 512] = OB[h].astype(F32).reshape(64, 512)
    for copy in sent:
        copy.wait_send()


def hand_out(fo_v, mo_v, vg_v, frames_out, memory_out, value_grad, sem):
    copies = [
        pltpu.make_async_copy(fo_v, frames_out, sem.at[0]),
        pltpu.make_async_copy(mo_v, memory_out, sem.at[1]),
        pltpu.make_async_copy(vg_v, value_grad, sem.at[2]),
    ]
    for copy in copies:
        copy.start()
    for copy in copies:
        copy.wait()


def on_device(
    frames, memory_in, lengths, ln_gain, w_query, w_key, w_value, w_out, grad_frames, grad_memory
):
    hbm = pl.BlockSpec(memory_space=pltpu.HBM)
    place = functools.partial(pltpu.with_memory_space_constraint, memory_space=pltpu.HBM)
    any_spec = pl.BlockSpec(memory_space=pl.ANY)
    vmem = pltpu.VMEM
    scratch = [
        vmem((4, 4, 4, 2, 32, 512), BF16),
        vmem((2, 2, 4, 2, 32, 512), BF16),
        vmem((128, 1024), BF16),
        vmem((8, 1024), BF16),
        vmem((8, 1024), BF16),
        vmem((2, 160, 1024), BF16),
        vmem((2, 2, 144, 512), BF16),
        vmem((2, 16, 1024), BF16),
        vmem((2, 160, 1024), BF16),
        vmem((2, 4, 4, 32, 384), BF16),
        vmem((2, 160, 144), F32),
        vmem((2, 4, 320, 128), BF16),
        vmem((2, 4, 144, 128), BF16),
        vmem((2, 4, 320, 128), BF16),
        vmem((2, 4, 320, 144), BF16),
        vmem((2, 4, 144, 128), BF16),
        vmem((384, 512), BF16),
        vmem((2, 4, 144, 128), BF16),
        vmem((2, 144, 512), BF16),
        vmem((2, 144, 512), BF16),
        vmem((2, 4, 4, 32, 512), BF16),
        vmem((2, 2, 2, 32, 512), BF16),
        vmem((2, 2, 2, 32, 512), BF16),
        vmem((2, 2, 2, 32, 512), BF16),
        vmem((2, 2, 2, 32, 512), BF16),
        vmem((2, 4, 2, 16, 512), BF16),
        vmem((2, 4, 2, 16, 512), F32),
        vmem((4, 4, 16, 512), BF16),
        vmem((4, 16, 512), BF16),
        vmem((2, 4, 16, 512), BF16),
        vmem((1, 1024), F32),
        pltpu.SemaphoreType.DMA((N_REMOTE,)),
        pltpu.SemaphoreType.DMA((N_REMOTE,)),
        pltpu.SemaphoreType.DMA((N_LOCAL,)),
        pltpu.SemaphoreType.REGULAR((4, 2)),
    ]
    shapes = (
        jax.ShapeDtypeStruct((128, 1024), BF16),
        jax.ShapeDtypeStruct((8, 1024), BF16),
        jax.ShapeDtypeStruct((64, 1024), F32),
    )
    results = pl.pallas_call(
        kernel,
        out_shape=shapes,
        in_specs=[hbm, hbm, pl.BlockSpec(memory_space=pltpu.SMEM)] + [hbm] * 7,
        out_specs=(pl.BlockSpec(memory_space=vmem),) * 3,
        scratch_shapes=scratch,
        compiler_params=pltpu.CompilerParams(
            collective_id=0, has_side_effects=True, vmem_limit_bytes=40 * 1024 * 1024
        ),
    )(
        place(frames.reshape(128, 1024)), place(memory_in.reshape(8, 1024)), lengths,
        place(ln_gain.reshape(1, 1024)), place(w_query), place(w_key), place(w_value),
        place(w_out), place(grad_frames.reshape(128, 1024)), place(grad_memory.reshape(8, 1024)),
    )
    frames_out, memory_out, value_grad = pl.pallas_call(
        hand_out,
        out_shape=shapes,
        in_specs=[any_spec] * 3,
        out_specs=(any_spec,) * 3,
        scratch_shapes=[pltpu.SemaphoreType.DMA((3,))],
        compiler_params=pltpu.CompilerParams(vmem_limit_bytes=1024 * 1024),
    )(*results)
    return (frames_out.reshape(frames.shape), memory_out.reshape(memory_in.shape), value_grad)


def solution(mesh):
    return jax.shard_map(
        on_device,
        mesh=mesh,
        in_specs=(
            P("fsdp", "seg", None, None),
            P("fsdp", "seg", None),
            P("fsdp"),
            P(),
            P("fsdp", None),
            P("fsdp", None),
            P("fsdp", None),
            P("fsdp", None),
            P("fsdp", "seg", None, None),
            P("fsdp", "seg", None),
        ),
        out_specs=(P("fsdp", "seg", None, None), P("fsdp", "seg", None), P("fsdp", None)),
        check_vma=False,
    )
```

```python
import functools

import jax
import jax.numpy as jnp
from jax import lax
from jax.experimental import pallas as pl
from jax.experimental.pallas import tpu as pltpu
from jax.sharding import PartitionSpec as P

F32 = jnp.float32
BF16 = jnp.bfloat16
MESH = pl.DeviceIdType.MESH
EPSILON = 1e-05
MASKED = -1e30
OUT, KEY, QUERY, VALUE = 0, 1, 2, 3
N_REMOTE = 192
N_LOCAL = 20


def mm(a, b):
    return jnp.dot(a, b, preferred_element_type=F32)


def kernel(
    frames, memory, lengths, gain, w_query, w_key, w_value, w_out, grad_frames, grad_memory,
    fo_v, mo_v, vg_v,
    W, WO2, fin, mem, gmem, E, U, L, X, XT, bias, K, Q, V, PT, GA, GV, ATT, PP, PPR,
    G, RA1, RA2A, RA2B, SA, RS, RF, RZ, ZQ, OB, gain_v,
    send_sem, recv_sem, local_sem, token_sem,
):
    seg = lax.axis_index("seg")
    fsdp = lax.axis_index("fsdp")
    core = lax.rem(seg, 2)
    z = lax.div(seg, 2)
    x = lax.rem(fsdp, 4)
    y = lax.div(fsdp, 4)
    other = 1 - core
    quad = lax.div(z, 4)
    place = lax.rem(z, 4)

    def wrap(a, by, n=4):
        return lax.rem(a + by + n, n)

    def device(dx=0, dy=0, dz=0, flip=False, quad_by=None):
        c = other if flip else core
        if quad_by is None:
            zz = wrap(z, dz, 16)
        else:
            zz = quad * 4 + wrap(place, quad_by)
        return (zz * 2 + c, wrap(y, dy) * 4 + wrap(x, dx))

    counter = [0]

    def remote(src, dst, to):
        i = counter[0]
        counter[0] += 1
        copy = pltpu.make_async_remote_copy(
            src_ref=src, dst_ref=dst, send_sem=send_sem.at[i], recv_sem=recv_sem.at[i],
            device_id=to, device_id_type=MESH,
        )
        copy.start()
        sent.append(copy)
        return copy

    sent = []
    lcounter = [0]

    def local(src, dst):
        i = lcounter[0]
        lcounter[0] += 1
        copy = pltpu.make_async_copy(src, dst, local_sem.at[i])
        copy.start()
        return copy

    weights = (w_out, w_key, w_query, w_value)
    own_columns = pl.ds(pl.multiple_of(core * 512, 512), 512)
    own = []
    for m in range(4):
        own.append([
            local(weights[m].at[pl.ds(32 * d, 32), own_columns], W.at[m, y, x, d])
            for d in range(2)
        ])
    in_frames = local(frames, fin)
    in_gain = local(gain, gain_v)
    in_mem = local(memory, mem)
    in_gmem = local(grad_memory, gmem)
    in_grad = [local(grad_frames.at[:, pl.ds(512 * h, 512)], U.at[core, h, pl.ds(0, 128)])
               for h in range(2)]

    partners = [device(dx=1), device(dx=-1), device(dy=1), device(dy=-1), device(flip=True),
                device(dz=1), device(dz=-1)]
    barrier = pltpu.get_barrier_semaphore()
    for partner in partners:
        pl.semaphore_signal(barrier, inc=1, device_id=partner, device_id_type=MESH)
    pl.semaphore_wait(barrier, len(partners))

    def pass_word(r):
        for i, s in enumerate((1, -1)):
            if r > 0:
                pl.semaphore_wait(token_sem.at[r - 1, i], 1)
            if r < 4:
                pl.semaphore_signal(token_sem.at[r, i], inc=1, device_id=device(dz=s),
                                    device_id_type=MESH)

    def first_to(d, s):
        return device(dx=s) if d == 0 else device(dy=s)

    def second_to(d, s):
        return device(dy=s) if d == 0 else device(dx=s)

    def piece(m, d, first=0, second=0, rows=None):
        dx, dy = (first, second) if d == 0 else (second, first)
        at = (m, wrap(y, dy), wrap(x, dx), d)
        return W.at[at if rows is None else at + (rows,)]

    flows = [(d, s) for s in (1, -1) for d in (0, 1)]
    direct, halves, forwarded, relayed = {}, {}, {}, {}

    def forward(m, d, kind):
        for s in (1, -1):
            ref = piece(m, d, first=kind)
            forwarded[m, d, s, kind] = remote(ref, ref, second_to(d, s))

    def stage0(m):
        for copy in own[m]:
            copy.wait()
        for d, s in flows:
            ref = piece(m, d)
            direct[m, d, s] = remote(ref, ref, first_to(d, s))
        for d in (0, 1):
            forward(m, d, 0)

    def stage1(m):
        for d, s in flows:
            direct[m, d, s].wait_recv()
            ref = piece(m, d, first=-s, rows=pl.ds(0 if s == 1 else 16, 16))
            halves[m, d, s] = remote(ref, ref, first_to(d, s))
        for d, s in flows:
            forward(m, d, -s)

    def stage2(m):
        for d in (0, 1):
            for s in (1, -1):
                halves[m, d, s].wait_recv()
            forward(m, d, 2)

    def stage3(m, kinds=(0, 1)):
        for i in kinds:
            for d, s in flows:
                kind = ((0, -1), (1, 2))[(1 - s) // 2][i]
                forwarded[m, d, s, kind].wait_recv()
                ref = piece(m, d, first=kind, second=-s)
                relayed[m, d, s, kind] = remote(ref, ref, second_to(d, s))

    def stage4(m):
        for d, s in flows:
            for kind in ((1, 2), (0, -1))[(1 - s) // 2]:
                forwarded[m, d, s, kind].wait_recv()
        for d, s in flows:
            for kind in ((0, -1), (1, 2))[(1 - s) // 2]:
                relayed[m, d, s, kind].wait_recv()

    for m in (OUT, KEY, QUERY):
        stage0(m)

    in_frames.wait()
    in_gain.wait()
    in_mem.wait()
    sums = []
    for t in range(8):
        rows = fin[16 * t:16 * t + 16, :].astype(F32)
        centred = rows - jnp.mean(rows, axis=-1, keepdims=True)
        var = jnp.mean(centred * centred, axis=-1, keepdims=True)
        normed = (centred * lax.rsqrt(var + EPSILON) * gain_v[...]).astype(BF16)
        E[core, 16 * t:16 * t + 16, :] = normed
        sums.append(jnp.mean(normed.astype(F32), axis=0, keepdims=True))
    zeros8 = jnp.zeros((8, 1024), F32)
    E[core, 128:144, :] = jnp.concatenate(sums + [zeros8], axis=0).astype(BF16)
    E[core, 144:160, :] = jnp.concatenate([mem[...].astype(F32), zeros8], axis=0).astype(BF16)
    rows_over = remote(E.at[core], E.at[core], device(flip=True))

    for m in (OUT, KEY, QUERY):
        stage1(m)

    in_gmem.wait()
    for h in range(2):
        in_grad[h].wait()
        U[core, h, 128:144, :] = jnp.concatenate(
            [gmem[:, 512 * h:512 * h + 512].astype(F32), zeros8[:, :512]], axis=0).astype(BF16)
    grads_over = remote(U.at[core], U.at[core], device(flip=True))

    stage2(OUT)
    stage2(KEY)
    rows_over.wait_recv()
    tail_over = remote(E.at[1, 112:128], L.at[0], device(dz=1))
    bank_over = remote(E.at[1, 144:160], L.at[1], device(dz=1))

    slot = lax.broadcasted_iota(jnp.int32, (160, 144), 0)
    column = lax.broadcasted_iota(jnp.int32, (160, 144), 1)
    query_at = jnp.where(column < 128, column // 16, column - 128)
    key_at = jnp.where(slot < 144, slot // 16 - 1, slot - 152)
    reach = jnp.where(slot < 144, 1, 8)
    newest = jnp.where(slot < 144, 0, 1)
    back = query_at - key_at
    for g in range(2):
        base = (2 * z + g) * 8
        valid = (back >= newest) & (back <= reach) & (key_at + base >= 0)
        bias[g] = jnp.where(valid, 0.0, MASKED).astype(F32)

    X[0, 16:144, :] = E[0, 0:128, :]
    X[1, 16:144, :] = E[1, 0:128, :]
    X[1, 0:16, :] = E[0, 112:128, :]
    bank0 = E[0, 144:160, :].astype(F32)[:8]
    bank1 = E[1, 144:160, :].astype(F32)[:8]
    X[1, 144:160, :] = jnp.concatenate([bank0, bank1], axis=0).astype(BF16)


    tail_over.wait_recv()
    bank_over.wait_recv()
    X[0, 0:16, :] = L[0]
    X[0, 144:160, :] = jnp.concatenate([L[1].astype(F32)[:8], bank0], axis=0).astype(BF16)
    for k in range(4):
        block = X[:, :, 256 * k:256 * k + 256].reshape(320, 256).astype(F32)
        block = jnp.concatenate([block, jnp.zeros((64, 256), F32)], axis=0).T.astype(BF16)
        for i in range(4):
            XT[0, k, i] = block[64 * i:64 * i + 32]
            XT[1, i, k] = block[64 * i + 32:64 * i + 64]

    stage2(QUERY)
    stage3(OUT)
    stage3(KEY)
    stage4(OUT)
    pass_word(0)
    out_over = remote(W.at[OUT, pl.ds(2 * other, 2)], WO2.at[core], device(flip=True))
    out_here = local(W.at[OUT, pl.ds(2 * core, 2)], WO2.at[core])
    stage3(QUERY)
    stage0(VALUE)
    pass_word(1)

    def live_of(g, shape):
        r = lax.broadcasted_iota(jnp.int32, shape, 0)
        at = jnp.where(r < 128, r // 16, r - 128)
        return jnp.where((2 * z + g) * 8 + at < lengths[0], 1.0, 0.0).astype(F32)

    low = lax.broadcasted_iota(jnp.int32, (1, 128), 1) < 64

    def split_heads(dst, value, g, p):
        dst[g, p, 0:160, :] = jnp.where(low, value, 0.0).astype(BF16)
        dst[g, p, 160:320, :] = jnp.where(low, 0.0, value).astype(BF16)

    def project_keys(m, dst):
        rows = X[...].reshape(320, 1024)
        for n in range(2):
            w = W[m, :, :, :, :, 256 * n:256 * n + 256].reshape(1024, 256)
            out = mm(rows, w)
            for g in range(2):
                for p in range(2):
                    split_heads(dst, out[160 * g:160 * g + 160, 128 * p:128 * p + 128], g, 2 * n + p)

    stage4(KEY)
    project_keys(KEY, K)
    pass_word(2)
    grads_over.wait_recv()
    out_here.wait()
    out_over.wait_recv()
    for g in range(2):
        ga = jnp.zeros((144, 512), F32)
        for h in range(2):
            w = WO2[h].reshape(512, 512)
            ga = ga + lax.dot_general(
                U[g, h], w, (((1,), (1,)), ((), ())), preferred_element_type=F32)
        ga = (ga * live_of(g, (144, 1))).astype(BF16)
        for p in range(4):
            GA[g, p] = ga[:, 128 * p:128 * p + 128]
    stage4(QUERY)
    query_rows = E[:, 0:144, :].reshape(288, 1024)
    for n in range(2):
        w = W[QUERY, :, :, :, :, 256 * n:256 * n + 256].reshape(1024, 256)
        out = mm(query_rows, w).astype(BF16)
        for g in range(2):
            for p in range(2):
                Q[g, 2 * n + p] = out[144 * g:144 * g + 144, 128 * p:128 * p + 128]

    stage1(VALUE)

    def attend(i, carry):
        g = lax.div(i, 4)
        p = lax.rem(i, 4)
        scores = lax.dot_general(
            K[g, p], Q[g, p], (((1,), (1,)), ((), ())), preferred_element_type=F32)
        for h in range(2):
            s = scores[160 * h:160 * h + 160] * 0.125 + bias[g]
            e = jnp.exp(s - jnp.max(s, axis=0, keepdims=True))
            total = jnp.sum(e, axis=0, keepdims=True)
            PT[g, p, 160 * h:160 * h + 160, :] = (e / total).astype(BF16)
        return carry

    lax.fori_loop(0, 8, attend, 0)

    pass_word(3)
    stage2(VALUE)
    pass_word(4)
    for g in range(2):
        for p in range(4):
            both = mm(PT[g, p], GA[g, p])
            GV[160 * g:160 * g + 160, 128 * p:128 * p + 128] = jnp.where(
                low, both[0:160], both[160:320]).astype(BF16)
    GV[320:384, :] = jnp.zeros((64, 512), BF16)

    def a_to(d, s):
        return device(dy=s) if d == 0 else device(dx=s)

    a_at = (y, x)
    b_at = (x, y)
    ways = [(d, s) for s in (1, -1) for d in (0, 1)]
    half_of = {1: 0, -1: 1}

    def g_part(d, by, h):
        return (d, wrap(a_at[d], by), pl.ds(2 * h, 2))

    a1, a2a, a2b = {}, {}, {}
    for by in (2, 1, -1, 0):
        rows = jnp.concatenate(
            [XT[d, wrap(a_at[d], by)].reshape(128, 384) for d in range(2)], axis=0)
        block = mm(rows, GV[...]).astype(BF16)
        for d in range(2):
            G[d, wrap(a_at[d], by)] = block[128 * d:128 * d + 128].reshape(4, 32, 512)
        if by == 2:
            for d, s in ways:
                h = half_of[s]
                a1[d, s] = remote(G.at[g_part(d, 2, h)], RA1.at[d, h], a_to(d, s))
        elif by != 0:
            for d in range(2):
                h = half_of[by]
                a2b[d, by] = remote(G.at[g_part(d, by, 1 - h)], RA2B.at[d, h], a_to(d, by))
    for d, s in ways:
        h = half_of[s]
        a1[d, s].wait_recv()
        SA[d, h] = (G[g_part(d, s, h)].astype(F32) + RA1[d, h].astype(F32)).astype(BF16)
        a2a[d, s] = remote(SA.at[d, h], RA2A.at[d, h], a_to(d, s))

    stage3(VALUE)

    for d in range(2):
        for s in (1, -1):
            a2a[d, s].wait_recv()
            a2b[d, s].wait_recv()
        for h in range(2):
            total = (G[g_part(d, 0, h)].astype(F32) + RA2A[d, h].astype(F32)
                     + RA2B[d, 1 - h].astype(F32))
            RF[d, 2 * h:2 * h + 2] = total.reshape(2, 2, 16, 512)
            RS[d, 2 * h:2 * h + 2] = total.astype(BF16).reshape(2, 2, 16, 512)

    z1 = []
    for k in (2, 1, 3, 0):
        to_place = wrap(place, k)
        d = lax.div(to_place, 2)
        for o in (2, 1, 3, 0):
            if o == 0 and k == 0:
                continue
            along = x + d * (y - x)
            to_x = wrap(x, (1 - d) * o)
            to_y = wrap(y, d * o)
            to = ((quad * 4 + to_place) * 2 + core, to_y * 4 + to_x)
            z1.append(remote(RS.at[d, wrap(along, o), lax.rem(to_place, 2)], RZ.at[o, k], to))

    stage4(VALUE)
    project_keys(VALUE, V)

    for copy in z1:
        copy.wait_recv()
    own_d = lax.div(place, 2)
    part = RF[own_d, x + own_d * (y - x), lax.rem(place, 2)]
    for o in range(4):
        for k in range(4):
            if o or k:
                part = part + RZ[o, k].astype(F32)
    ZQ[quad] = part.astype(BF16)
    z2 = {s: remote(ZQ.at[quad], ZQ.at[quad], device(dz=4 * s)) for s in (1, -1)}

    def attended(i, carry):
        g = lax.div(i, 4)
        p = lax.rem(i, 4)
        ATT[g, p] = lax.dot_general(
            PT[g, p], V[g, p], (((0,), (0,)), ((), ())), preferred_element_type=F32).astype(BF16)
        return carry

    lax.fori_loop(0, 8, attended, 0)

    z3 = {}
    for s in (1, -1):
        z2[s].wait_recv()
        cols = pl.ds(256 * half_of[s], 256)
        ref = ZQ.at[wrap(quad, -s), :, cols]
        z3[s] = remote(ref, ref, device(dz=4 * s))

    def project(g, h):
        rows = jnp.concatenate([ATT[g, p] for p in range(4)], axis=1)
        return mm(rows, WO2[h].reshape(512, 512))

    for h in range(2):
        PP[h] = project(other, h).astype(BF16)
    projected_over = remote(PP, PPR, device(flip=True))

    for s in (1, -1):
        z3[s].wait_recv()
    done = ((ZQ[0].astype(F32) + ZQ[1].astype(F32)) + ZQ[2].astype(F32)) + ZQ[3].astype(F32)
    OB[core, place] = done.astype(BF16)
    mine = OB.at[core, place]
    z4 = [remote(mine, mine, device(quad_by=k)) for k in (1, 2, 3)]
    z4 += [remote(mine, mine, device(quad_by=k, flip=True)) for k in (0, 1, 2, 3)]

    projected_over.wait_recv()
    live = live_of(core, (144, 1))
    for h in range(2):
        cols = slice(512 * h, 512 * h + 512)
        out = (project(core, h) + PPR[h].astype(F32)) * live
        fo_v[:, cols] = (fin[:, cols].astype(F32) + out[0:128]).astype(BF16)
        mo_v[:, cols] = out[128:136].astype(BF16)

    for copy in z4:
        copy.wait_recv()
    for h in range(2):
        vg_v[:, 512 * h:512 * h + 512] = OB[h].astype(F32).reshape(64, 512)
    for copy in sent:
        copy.wait_send()


def hand_out(fo_v, mo_v, vg_v, frames_out, memory_out, value_grad, sem):
    copies = [
        pltpu.make_async_copy(fo_v, frames_out, sem.at[0]),
        pltpu.make_async_copy(mo_v, memory_out, sem.at[1]),
        pltpu.make_async_copy(vg_v, value_grad, sem.at[2]),
    ]
    for copy in copies:
        copy.start()
    for copy in copies:
        copy.wait()


def on_device(
    frames, memory_in, lengths, ln_gain, w_query, w_key, w_value, w_out, grad_frames, grad_memory
):
    hbm = pl.BlockSpec(memory_space=pltpu.HBM)
    place = functools.partial(pltpu.with_memory_space_constraint, memory_space=pltpu.HBM)
    any_spec = pl.BlockSpec(memory_space=pl.ANY)
    vmem = pltpu.VMEM
    scratch = [
        vmem((4, 4, 4, 2, 32, 512), BF16),
        vmem((2, 2, 4, 2, 32, 512), BF16),
        vmem((128, 1024), BF16),
        vmem((8, 1024), BF16),
        vmem((8, 1024), BF16),
        vmem((2, 160, 1024), BF16),
        vmem((2, 2, 144, 512), BF16),
        vmem((2, 16, 1024), BF16),
        vmem((2, 160, 1024), BF16),
        vmem((2, 4, 4, 32, 384), BF16),
        vmem((2, 160, 144), F32),
        vmem((2, 4, 320, 128), BF16),
        vmem((2, 4, 144, 128), BF16),
        vmem((2, 4, 320, 128), BF16),
        vmem((2, 4, 320, 144), BF16),
        vmem((2, 4, 144, 128), BF16),
        vmem((384, 512), BF16),
        vmem((2, 4, 144, 128), BF16),
        vmem((2, 144, 512), BF16),
        vmem((2, 144, 512), BF16),
        vmem((2, 4, 4, 32, 512), BF16),
        vmem((2, 2, 2, 32, 512), BF16),
        vmem((2, 2, 2, 32, 512), BF16),
        vmem((2, 2, 2, 32, 512), BF16),
        vmem((2, 2, 2, 32, 512), BF16),
        vmem((2, 4, 2, 16, 512), BF16),
        vmem((2, 4, 2, 16, 512), F32),
        vmem((4, 4, 16, 512), BF16),
        vmem((4, 16, 512), BF16),
        vmem((2, 4, 16, 512), BF16),
        vmem((1, 1024), F32),
        pltpu.SemaphoreType.DMA((N_REMOTE,)),
        pltpu.SemaphoreType.DMA((N_REMOTE,)),
        pltpu.SemaphoreType.DMA((N_LOCAL,)),
        pltpu.SemaphoreType.REGULAR((4, 2)),
    ]
    shapes = (
        jax.ShapeDtypeStruct((128, 1024), BF16),
        jax.ShapeDtypeStruct((8, 1024), BF16),
        jax.ShapeDtypeStruct((64, 1024), F32),
    )
    results = pl.pallas_call(
        kernel,
        out_shape=shapes,
        in_specs=[hbm, hbm, pl.BlockSpec(memory_space=pltpu.SMEM)] + [hbm] * 7,
        out_specs=(pl.BlockSpec(memory_space=vmem),) * 3,
        scratch_shapes=scratch,
        compiler_params=pltpu.CompilerParams(
            collective_id=0, has_side_effects=True, vmem_limit_bytes=40 * 1024 * 1024
        ),
    )(
        place(frames.reshape(128, 1024)), place(memory_in.reshape(8, 1024)), lengths,
        place(ln_gain.reshape(1, 1024)), place(w_query), place(w_key), place(w_value),
        place(w_out), place(grad_frames.reshape(128, 1024)), place(grad_memory.reshape(8, 1024)),
    )
    frames_out, memory_out, value_grad = pl.pallas_call(
        hand_out,
        out_shape=shapes,
        in_specs=[any_spec] * 3,
        out_specs=(any_spec,) * 3,
        scratch_shapes=[pltpu.SemaphoreType.DMA((3,))],
        compiler_params=pltpu.CompilerParams(vmem_limit_bytes=1024 * 1024),
    )(*results)
    return (frames_out.reshape(frames.shape), memory_out.reshape(memory_in.shape), value_grad)


def solution(mesh):
    return jax.shard_map(
        on_device,
        mesh=mesh,
        in_specs=(
            P("fsdp", "seg", None, None),
            P("fsdp", "seg", None),
            P("fsdp"),
            P(),
            P("fsdp", None),
            P("fsdp", None),
            P("fsdp", None),
            P("fsdp", None),
            P("fsdp", "seg", None, None),
            P("fsdp", "seg", None),
        ),
        out_specs=(P("fsdp", "seg", None, None), P("fsdp", "seg", None), P("fsdp", None)),
        check_vma=False,
    )
```
